32 devices in a mesh: grp: 2 (over y), fsdp: 8 (over z, x), seq: 2 (over core).
Axes of the slice: x: 2, y: 2, z: 4, core: 2. Of those that a mesh axis runs over, the one named last changes fastest.
Arguments:
- prompt_in: bfloat16 [2, 1024, 768], P('grp', ('fsdp', 'seq')), may hold values from -6 to 6
- cont_in: bfloat16 [2, 16, 1024, 768], P('grp', 'fsdp', 'seq'), may hold values from -6 to 6
- enc_in: bfloat16 [2, 1024, 768], P('grp', ('fsdp', 'seq')), may hold values from -6 to 6
- prefix: int32 [2, 16], P('grp', 'fsdp'), may hold values from 1 to 1024, as said below
- cot_prompt: bfloat16 [2, 1024, 768], P('grp', ('fsdp', 'seq')), may hold values from -6 to 6
- cot_cont: bfloat16 [2, 16, 1024, 768], P('grp', 'fsdp', 'seq'), may hold values from -6 to 6
- w_qkv: bfloat16 [768, 2304], P('fsdp'), may hold values from -0.3125 to 0.3125
- w_attn_out: bfloat16 [768, 768], P('fsdp'), may hold values from -0.75 to 0.75
- w_cross_q: bfloat16 [768, 768], P('fsdp'), may hold values from -0.3125 to 0.3125
- w_cross_kv: bfloat16 [768, 1536], P('fsdp'), may hold values from -0.3125 to 0.3125
- w_cross_out: bfloat16 [768, 768], P('fsdp'), may hold values from -0.75 to 0.75
- w_ffn_in: bfloat16 [768, 3072], P('fsdp'), may hold values from -0.21875 to 0.21875
- w_ffn_out: bfloat16 [3072, 768], P('fsdp'), may hold values from -0.109375 to 0.109375
- norm_gain: bfloat16 [3, 768], P(None, 'fsdp'), may hold values from 0.099609375 to 1.8984375
- norm_bias: bfloat16 [3, 768], P(None, 'fsdp'), may hold values from -3 to 3
Outputs:
- out_prompt: bfloat16 [2, 1024, 768], P('grp', ('fsdp', 'seq'))
- out_cont: bfloat16 [2, 16, 1024, 768], P('grp', 'fsdp', 'seq')
- grad_prompt: float32 [2, 1024, 768], P('grp', ('fsdp', 'seq'))
- grad_cont: float32 [2, 16, 1024, 768], P('grp', 'fsdp', 'seq')
- grad_enc: float32 [2, 1024, 768], P('grp', ('fsdp', 'seq'))
- grad_w_qkv: float32 [768, 2304], P('fsdp')
- grad_w_attn_out: float32 [768, 768], P('fsdp')
- grad_w_cross_q: float32 [768, 768], P('fsdp')
- grad_w_cross_kv: float32 [768, 1536], P('fsdp')
- grad_w_cross_out: float32 [768, 768], P('fsdp')
- grad_w_ffn_in: float32 [768, 3072], P('fsdp')
- grad_w_ffn_out: float32 [3072, 768], P('fsdp')
- grad_norm_gain: float32 [3, 768], P(None, 'fsdp')
- grad_norm_bias: float32 [3, 768], P(None, 'fsdp')
The draws below stay inside these ranges and needn't reach their ends.
Inputs may be any that keep to these rules, and one draw needn't show every extreme that they name: Continuation c sees prompt positions below prefix[c]; in every group some continuation sees the whole prompt of 1024 tokens.
All inputs are finite; a program needn't handle non-finite values.
Results may differ from the reference program's by a relative error of at most 0.034.
The reference program's roundings to bfloat16 on the way count: a program that leaves them out, or rounds other values in their place, can miss the bound.
Values may be sent and summed in bfloat16 or wider, within the bound.
A program may use at most 448 MiB of HBM per device.

```python
import jax
import jax.numpy as jnp
from jax import lax

D = 768
FF = 3072
HEADS = 12
HEAD_DIM = 64
PROMPT = 1024
CONT_LEN = 1024
ENC_LEN = 1024
MICRO = 2
GROUPS = 2
CONTS = 16
N_FSDP = 8


def draw_prefix(key, part):
    reaches = jax.random.randint(key, (GROUPS, CONTS), 1, PROMPT + 1, dtype=jnp.int32)
    return reaches.at[:, 0].set(PROMPT)


def shard_levels(own_key, extent, shards, low, largest):
    level = 1.0
    for dim, blocks in shards:
        heights = jax.random.uniform(jax.random.fold_in(jax.random.fold_in(own_key, 6), dim), (blocks,), jnp.float32, low / len(shards), largest / len(shards))
        level = level * jnp.repeat(jnp.exp(heights), extent[dim] // blocks).reshape((-1,) + (1,) * (len(extent) - 1 - dim))
    return level


def scatter_about(own_key, extent, deviation, bound, pieces=(), kind=jnp.bfloat16):
    level = shard_levels(own_key, extent, pieces, -0.22, 0.18) if pieces else 1.0
    entries = jax.random.normal(own_key, extent, jnp.float32) * deviation * level
    return jnp.minimum(jnp.maximum(entries, -bound), bound).astype(kind)


def setup_inputs(seed: int = 0) -> dict:
    splits = jax.random.split(jax.random.key(seed), 16)
    return {
        "prompt_in": scatter_about(splits[0], (GROUPS, PROMPT, D), 1.0, 6.0, ((0, 2), (1, 16))),
        "cont_in": scatter_about(splits[1], (GROUPS, CONTS, CONT_LEN, D), 1.0, 6.0, ((0, 2), (1, 8), (2, 2))),
        "enc_in": scatter_about(splits[2], (GROUPS, ENC_LEN, D), 1.0, 6.0, ((0, 2), (1, 16))),
        "prefix": draw_prefix(jax.random.fold_in(splits[15], 71), 0),
        "cot_prompt": scatter_about(splits[4], (GROUPS, PROMPT, D), 1.0, 6.0, ((0, 2), (1, 16))),
        "cot_cont": scatter_about(splits[5], (GROUPS, CONTS, CONT_LEN, D), 1.0, 6.0, ((0, 2), (1, 8), (2, 2))),
        "w_qkv": scatter_about(splits[6], (D, 3 * D), (D // 2) ** -0.5, 0.3125, ((0, 8),)),
        "w_attn_out": scatter_about(splits[7], (D, D), 64 ** -0.5, 0.75, ((0, 8),)),
        "w_cross_q": scatter_about(splits[8], (D, D), (D // 2) ** -0.5, 0.3125, ((0, 8),)),
        "w_cross_kv": scatter_about(splits[9], (D, 2 * D), (D // 2) ** -0.5, 0.3125, ((0, 8),)),
        "w_cross_out": scatter_about(splits[10], (D, D), 64 ** -0.5, 0.75, ((0, 8),)),
        "w_ffn_in": scatter_about(splits[11], (D, FF), D ** -0.5, 0.21875, ((0, 8),)),
        "w_ffn_out": scatter_about(splits[12], (FF, D), FF ** -0.5, 0.109375, ((0, 8),)),
        "norm_gain": jnp.clip(1.0 + 0.18 * jax.random.normal(splits[13], (3, D), jnp.float32), 0.099609375, 1.8984375).astype(jnp.bfloat16),
        "norm_bias": scatter_about(splits[14], (3, D), 0.5, 3.0, ((1, 8),)),
    }


@jax.custom_vjp
def low(v):
    return lax.optimization_barrier(v.astype(jnp.bfloat16)).astype(jnp.float32)

@jax.custom_vjp
def low_back(v):
    return v

def low_keep(v):
    return (low(v), None)

def low_pass(kept, grad):
    return (grad,)

def back_keep(v):
    return (v, None)

def back_low(kept, grad):
    return (low(grad),)
low.defvjp(low_keep, low_pass)
low_back.defvjp(back_keep, back_low)
SCALE = 0.125
EPS = 1e-05

def matmul_high(left, right):
    return jnp.dot(left, right, precision=lax.Precision.HIGHEST)

def norm_rows(resid, gain, shift):
    average = lax.optimization_barrier(jnp.mean(resid, axis=-1, keepdims=True))
    centred = resid - average
    variance = lax.optimization_barrier(jnp.mean(centred * centred, axis=-1, keepdims=True))
    return centred * lax.rsqrt(variance + EPS) * gain + shift

def attend_block(queries, key_rows, value_rows, allowed):
    scores = jnp.einsum('bhe,khe->hbk', queries, key_rows, precision=lax.Precision.HIGHEST) * SCALE
    scores = jnp.where(allowed[None], low_back(scores), -jnp.inf)
    prob_rows = jax.nn.softmax(scores, axis=-1)
    return jnp.einsum('hbk,khe->bhe', low(prob_rows), value_rows, precision=lax.Precision.HIGHEST)

def self_attention(queries, key_rows, value_rows, reach_all):
    prompt_q = queries[:PROMPT]
    prompt_k = key_rows[:PROMPT]
    prompt_v = value_rows[:PROMPT]
    head_shape = (reach_all.shape[0], CONT_LEN, HEADS, HEAD_DIM)
    cont_q = queries[PROMPT:].reshape(head_shape)
    cont_k = key_rows[PROMPT:].reshape(head_shape)
    cont_v = value_rows[PROMPT:].reshape(head_shape)
    key_place = jnp.arange(PROMPT, dtype=jnp.int32)
    local_place = jnp.arange(CONT_LEN, dtype=jnp.int32)

    def prompt_block(block_index):
        block_q = lax.dynamic_slice_in_dim(prompt_q, block_index * CONT_LEN, CONT_LEN)
        allowed = key_place[None, :] <= (block_index * CONT_LEN + local_place)[:, None]
        return attend_block(block_q, prompt_k, prompt_v, allowed)

    def cont_block(inputs):
        block_q, block_k, block_v, reach_len = inputs
        seen = jnp.broadcast_to(key_place[None, :] < reach_len, (CONT_LEN, PROMPT))
        allowed = jnp.concatenate([seen, local_place[None, :] <= local_place[:, None]], 1)
        return attend_block(block_q, jnp.concatenate([prompt_k, block_k], 0), jnp.concatenate([prompt_v, block_v], 0), allowed)
    prompt_out = lax.map(jax.checkpoint(prompt_block), jnp.arange(PROMPT // CONT_LEN, dtype=jnp.int32))
    cont_out = lax.map(jax.checkpoint(cont_block), (cont_q, cont_k, cont_v, reach_all))
    return jnp.concatenate([prompt_out.reshape(PROMPT, HEADS, HEAD_DIM), cont_out.reshape(-1, HEADS, HEAD_DIM)], 0)

def layer(params, prompt_x, cont_x, encoder, reach_all):
    w_qkv, w_attn_out, w_cross_q, w_cross_kv, w_cross_out, w_ffn_in, w_ffn_out, gain_rows, bias_rows = params
    inputs = jnp.concatenate([prompt_x, cont_x.reshape(-1, D)], 0)
    row_total = inputs.shape[0]
    qkv_rows = low(low_back(matmul_high(inputs, w_qkv))).reshape(row_total, 3, HEADS, HEAD_DIM)
    self_att = self_attention(qkv_rows[:, 0], qkv_rows[:, 1], qkv_rows[:, 2], reach_all)
    self_att = low(low_back(self_att.reshape(row_total, D)))
    first_out = norm_rows(inputs + low_back(matmul_high(self_att, w_attn_out)), gain_rows[0], bias_rows[0])
    cross_q = low(low_back(matmul_high(low(first_out), w_cross_q)))
    cross_q = cross_q.reshape(row_total // CONT_LEN, CONT_LEN, HEADS, HEAD_DIM)
    cross_kv = low(low_back(matmul_high(encoder, w_cross_kv))).reshape(ENC_LEN, 2, HEADS, HEAD_DIM)
    every_key = (jnp.arange(ENC_LEN, dtype=jnp.int32) >= 0)[None, :]

    def cross_block(block_q):
        return attend_block(block_q, cross_kv[:, 0], cross_kv[:, 1], every_key)
    cross_att = lax.map(jax.checkpoint(cross_block), cross_q)
    cross_att = low(low_back(cross_att.reshape(row_total, D)))
    second = norm_rows(first_out + low_back(matmul_high(cross_att, w_cross_out)), gain_rows[1], bias_rows[1])
    pre_act = low_back(matmul_high(low(second), w_ffn_in))
    activated = low(jax.nn.gelu(pre_act, approximate=False))
    third_out = norm_rows(second + low_back(matmul_high(activated, w_ffn_out)), gain_rows[2], bias_rows[2])
    return (third_out[:PROMPT], third_out[PROMPT:].reshape(cont_x.shape))

def reference(prompt_in, cont_in, enc_in, prefix, cot_prompt, cot_cont, w_qkv, w_attn_out, w_cross_q, w_cross_kv, w_cross_out, w_ffn_in, w_ffn_out, norm_gain, norm_bias):
    params = tuple((item.astype(jnp.float32) for item in (w_qkv, w_attn_out, w_cross_q, w_cross_kv, w_cross_out, w_ffn_in, w_ffn_out, norm_gain, norm_bias)))
    grad_params = tuple((jnp.zeros_like(item) for item in params))
    out_prompt, out_cont, grad_prompt, grad_cont, grad_enc = ([], [], [], [], [])
    for group_index in range(GROUPS):
        prompt_x = prompt_in[group_index].astype(jnp.float32)
        conts = cont_in[group_index].astype(jnp.float32).reshape(N_FSDP, MICRO, CONT_LEN, D)
        reaches = prefix[group_index].reshape(N_FSDP, MICRO)
        encoder = enc_in[group_index].astype(jnp.float32)
        cot_p = cot_prompt[group_index].astype(jnp.float32)
        cot_c = cot_cont[group_index].astype(jnp.float32).reshape(N_FSDP, MICRO, CONT_LEN, D)
        prompt_sum = jnp.zeros_like(prompt_x)
        enc_sum = jnp.zeros_like(encoder)
        cont_outs, cont_grads = ([], [])
        prompt_first = None
        for micro_index in range(MICRO):
            reach_all = reaches[:, micro_index]

            def forward(weights, prompt_rows, cont_rows, enc_rows):
                return layer(weights, prompt_rows, cont_rows, enc_rows, reach_all)
            (prompt_y, cont_y), pull_back = jax.vjp(forward, params, prompt_x, conts[:, micro_index], encoder)
            prompt_cot = cot_p if micro_index == 0 else jnp.zeros_like(cot_p)
            d_params, d_prompt, d_cont, d_enc = pull_back((prompt_cot, cot_c[:, micro_index]))
            grad_params = tuple((left + right for left, right in zip(grad_params, d_params)))
            prompt_sum = prompt_sum + d_prompt
            enc_sum = enc_sum + d_enc
            cont_outs.append(cont_y)
            cont_grads.append(d_cont)
            if micro_index == 0:
                prompt_first = prompt_y
        out_prompt.append(prompt_first.astype(jnp.bfloat16))
        out_cont.append(jnp.stack(cont_outs, 1).reshape(CONTS, CONT_LEN, D).astype(jnp.bfloat16))
        grad_prompt.append(prompt_sum)
        grad_cont.append(jnp.stack(cont_grads, 1).reshape(CONTS, CONT_LEN, D))
        grad_enc.append(enc_sum)
    return (jnp.stack(out_prompt), jnp.stack(out_cont), jnp.stack(grad_prompt), jnp.stack(grad_cont), jnp.stack(grad_enc), grad_params[0], grad_params[1], grad_params[2], grad_params[3], grad_params[4], grad_params[5], grad_params[6], grad_params[7], grad_params[8])
```

```python
import jax
import jax.numpy as jnp
from jax import lax
from jax.sharding import PartitionSpec as P

HEAD_DIM = 64
SCALE = 0.125
EPS = 1e-05
MASKED = -1e30
BF = jnp.bfloat16
F32 = jnp.float32


def mm(a, b):
    return jnp.dot(a, b, preferred_element_type=F32)


def mm_tn(a, b):
    return lax.dot_general(a, b, (((0,), (0,)), ((), ())), preferred_element_type=F32)


def mm_nt(a, b):
    return lax.dot_general(a, b, (((1,), (1,)), ((), ())), preferred_element_type=F32)


def swap(value, axis):
    return lax.ppermute(value, axis, [(0, 1), (1, 0)])


def half_rows(value):
    half = value.shape[0] // 2
    return lax.dynamic_slice_in_dim(value, lax.axis_index("seq") * half, half, 0)


def gather_rows(shard):
    return lax.all_gather(half_rows(shard), ("fsdp", "seq"), axis=0, tiled=True)


def both_halves(mine):
    other = swap(mine, "seq")
    first = lax.axis_index("seq") == 0
    low = jnp.where(first, mine, other)
    high = jnp.where(first, other, mine)
    return low, high


def reduce_rows(grad):
    part = lax.psum_scatter(grad.astype(BF), ("fsdp", "seq"), scatter_dimension=0, tiled=True)
    total = (part.astype(F32) + swap(part, "grp").astype(F32)).astype(BF)
    return jnp.concatenate(both_halves(total), 0).astype(F32)


def norm_stats(resid):
    average = jnp.mean(resid, axis=-1, keepdims=True)
    centred = resid - average
    variance = jnp.mean(centred * centred, axis=-1, keepdims=True)
    scale = lax.rsqrt(variance + EPS)
    return centred * scale, scale


def norm_back(grad, hat, scale, gain):
    weighted = grad * gain
    first = jnp.mean(weighted, axis=-1, keepdims=True)
    second = jnp.mean(weighted * hat, axis=-1, keepdims=True)
    back = scale * (weighted - first - hat * second)
    return back, jnp.sum(grad * hat, axis=0), jnp.sum(grad, axis=0)


def heads(value):
    return value.reshape(value.shape[0], -1, HEAD_DIM)


def attend(queries, keys, values, allowed):
    scores = jnp.einsum("qhe,khe->hqk", heads(queries), heads(keys), preferred_element_type=F32)
    scores = jnp.where(allowed, scores * SCALE, MASKED)
    top = jnp.max(scores, axis=-1, keepdims=True)
    raised = jnp.exp(scores - top)
    total = jnp.sum(raised, axis=-1, keepdims=True)
    out = jnp.einsum(
        "hqk,khe->qhe", raised.astype(BF), heads(values), preferred_element_type=F32
    )
    out = out / jnp.transpose(total, (1, 0, 2))
    return out.reshape(queries.shape).astype(BF), top + jnp.log(total)


def attend_back(queries, keys, values, allowed, out, grad, log_sum):
    scores = jnp.einsum("qhe,khe->hqk", heads(queries), heads(keys), preferred_element_type=F32)
    prob = jnp.exp(jnp.where(allowed, scores * SCALE, MASKED) - log_sum)
    grad_prob = jnp.einsum("qhe,khe->hqk", heads(grad), heads(values), preferred_element_type=F32)
    delta = jnp.sum(heads(grad).astype(F32) * heads(out).astype(F32), axis=-1).T[..., None]
    grad_score = (prob * (grad_prob - delta)).astype(BF)
    grad_q = jnp.einsum("hqk,khe->qhe", grad_score, heads(keys), preferred_element_type=F32)
    grad_k = jnp.einsum("hqk,qhe->khe", grad_score, heads(queries), preferred_element_type=F32)
    grad_v = jnp.einsum("hqk,qhe->khe", prob.astype(BF), heads(grad), preferred_element_type=F32)
    return (
        (grad_q * SCALE).reshape(queries.shape),
        (grad_k * SCALE).reshape(keys.shape),
        grad_v.reshape(values.shape),
    )


def self_masks(prompt_len, cont_len, reach):
    key = lax.iota(jnp.int32, prompt_len)[None, :]
    seen = jnp.broadcast_to(key < reach, (cont_len, prompt_len))
    own = lax.iota(jnp.int32, cont_len)
    return jnp.concatenate([seen, own[None, :] <= own[:, None]], 1)[None]


def self_forward(joined, prompt_kv, reach, place, conts):
    width = joined.shape[2] // 3
    cont_len = conts[2]
    half = cont_len // 2
    prompt_len = prompt_kv.shape[0]
    outs, sums = [], []
    for c in range(conts[1]):
        rows = joined[:, c * half : (c + 1) * half].reshape(cont_len, -1)
        keys = jnp.concatenate([prompt_kv[:, :width], rows[:, width : 2 * width]], 0)
        values = jnp.concatenate([prompt_kv[:, width:], rows[:, 2 * width :]], 0)
        out, log_sum = attend(rows[:, :width], keys, values, self_masks(prompt_len, cont_len, reach[c]))
        outs.append(out.reshape(2, half, width))
        sums.append(log_sum)
    rows = joined[:, conts[1] * half :].reshape(-1, 3 * width)
    allowed = lax.iota(jnp.int32, prompt_len)[None, None, :] <= place[None, :, None]
    out, log_sum = attend(rows[:, :width], prompt_kv[:, :width], prompt_kv[:, width:], allowed)
    outs.append(out.reshape(2, -1, width))
    sums.append(log_sum)
    return jnp.concatenate(outs, 1), tuple(sums)


def self_backward(joined, prompt_kv, reach, place, conts, out, grad, sums):
    width = joined.shape[2] // 3
    cont_len = conts[2]
    half = cont_len // 2
    prompt_len = prompt_kv.shape[0]
    pieces = []
    total_kv = 0.0
    for c in range(conts[1]):
        span = slice(c * half, (c + 1) * half)
        rows = joined[:, span].reshape(cont_len, -1)
        keys = jnp.concatenate([prompt_kv[:, :width], rows[:, width : 2 * width]], 0)
        values = jnp.concatenate([prompt_kv[:, width:], rows[:, 2 * width :]], 0)
        grad_q, grad_k, grad_v = attend_back(
            rows[:, :width],
            keys,
            values,
            self_masks(prompt_len, cont_len, reach[c]),
            out[:, span].reshape(cont_len, width),
            grad[:, span].reshape(cont_len, width),
            sums[c],
        )
        total_kv = total_kv + jnp.concatenate([grad_k[:prompt_len], grad_v[:prompt_len]], 1)
        piece = jnp.concatenate([grad_q, grad_k[prompt_len:], grad_v[prompt_len:]], 1)
        pieces.append(piece.astype(BF).reshape(2, half, 3 * width))
    start = conts[1] * half
    rows = joined[:, start:].reshape(-1, 3 * width)
    allowed = lax.iota(jnp.int32, prompt_len)[None, None, :] <= place[None, :, None]
    grad_q, grad_k, grad_v = attend_back(
        rows[:, :width],
        prompt_kv[:, :width],
        prompt_kv[:, width:],
        allowed,
        out[:, start:].reshape(-1, width),
        grad[:, start:].reshape(-1, width),
        sums[-1],
    )
    total_kv = total_kv + jnp.concatenate([grad_k, grad_v], 1)
    zero = jnp.zeros((2, rows.shape[0] // 2, 2 * width), BF)
    pieces.append(jnp.concatenate([grad_q.astype(BF).reshape(2, -1, width), zero], 2))
    return jnp.concatenate(pieces, 1), total_kv.astype(BF)


def cross_forward(queries, enc_kv):
    width = queries.shape[1]
    return attend(queries, enc_kv[:, :width], enc_kv[:, width:], True)


def cross_backward(queries, enc_kv, out, grad, log_sum):
    width = queries.shape[1]
    grad_q, grad_k, grad_v = attend_back(
        queries, enc_kv[:, :width], enc_kv[:, width:], True, out, grad, log_sum
    )
    return grad_q.astype(BF), jnp.concatenate([grad_k, grad_v], 1).astype(BF)


def exchange(value):
    return lax.all_to_all(value, "seq", split_axis=0, concat_axis=0, tiled=True)


def on_device(
    prompt_in,
    cont_in,
    enc_in,
    prefix,
    cot_prompt,
    cot_cont,
    w_qkv,
    w_attn_out,
    w_cross_q,
    w_cross_kv,
    w_cross_out,
    w_ffn_in,
    w_ffn_out,
    norm_gain,
    norm_bias,
):
    seq = lax.axis_index("seq")
    width = w_qkv.shape[1] // 3
    hg = width // 2
    shard = w_qkv.shape[0]
    rows_p = prompt_in.shape[1]
    count = cont_in.shape[1]
    half = cont_in.shape[2]
    rows_c = count * half
    conts = (rows_c, count, 2 * half)
    reach = prefix[0]

    own_cols = lax.dynamic_slice_in_dim(w_qkv.reshape(shard, 3, 2, hg), seq, 1, 2)
    wq = lax.all_gather(own_cols.reshape(shard, 3 * hg), "fsdp", axis=0, tiled=True)
    shared = lax.all_gather(
        jnp.concatenate([prompt_in[0], enc_in[0]], 0), ("fsdp", "seq"), axis=0
    )
    prompt_all = shared[:, :rows_p].reshape(-1, width)
    enc_all = shared[:, rows_p:].reshape(-1, width)
    norms = jnp.concatenate([norm_gain, norm_bias], 0).T
    norms = jnp.pad(norms, ((0, 0), (0, 128 - norms.shape[1])))
    mixed = gather_rows(jnp.concatenate([w_attn_out, w_cross_q, w_cross_out, w_cross_kv, norms], 1))
    wo = mixed[:, :width]
    wcq = mixed[:, width : 2 * width]
    wco = mixed[:, 2 * width : 3 * width]
    wckv = mixed[:, 3 * width : 5 * width]
    norms = mixed[:, 5 * width :].astype(F32).T
    w1 = gather_rows(w_ffn_in)
    w2 = gather_rows(w_ffn_out)

    mine = jnp.concatenate([cont_in[0].reshape(rows_c, width), prompt_in[0]], 0)
    x_low, x_high = both_halves(mine)
    x_all = jnp.stack([x_low, x_high], 0)
    joined = lax.dot_general(
        x_all, wq, (((2,), (0,)), ((), ())), preferred_element_type=F32
    ).astype(BF)
    prompt_kv = mm(prompt_all, wq[:, hg:]).astype(BF)
    place = lax.axis_index("fsdp") * (2 * rows_p) + lax.iota(jnp.int32, 2 * rows_p)
    att, sums = self_forward(joined, prompt_kv, reach, place, conts)
    att = att
    att_rows = exchange(att)
    proj = mm(att_rows[0], wo[:hg]) + mm(att_rows[1], wo[hg:])
    hat1, scale1 = norm_stats(mine.astype(F32) + proj)
    first = hat1 * norms[0] + norms[3]
    first_low = first.astype(BF)
    cq = mm(first_low, wcq).astype(BF)
    enc_kv = mm(enc_all, wckv).astype(BF)
    cross, cross_sum = cross_forward(cq, enc_kv)
    hat2, scale2 = norm_stats(first + mm(cross, wco))
    second = hat2 * norms[1] + norms[4]
    second_low = second.astype(BF)
    pre = mm(second_low, w1)
    gate = 0.5 * (1.0 + lax.erf(pre * 0.7071067811865476))
    act = (pre * gate).astype(BF)
    slope = (gate + pre * jnp.exp(-0.5 * pre * pre) * 0.3989422804014327).astype(BF)
    hat3, scale3 = norm_stats(second + mm(act, w2))
    third = (hat3 * norms[2] + norms[5]).astype(BF)

    cot = jnp.concatenate([cot_cont[0].reshape(rows_c, width), cot_prompt[0]], 0).astype(F32)
    grad3, gain3, bias3 = norm_back(cot, hat3, scale3, norms[2])
    low3 = grad3.astype(BF)
    g_w2 = reduce_rows(mm_tn(act, low3))
    grad_pre = (mm_nt(low3, w2) * slope.astype(F32)).astype(BF)
    g_w1 = reduce_rows(mm_tn(second_low, grad_pre))
    grad_second = grad3 + mm_nt(grad_pre, w1)
    grad2, gain2, bias2 = norm_back(grad_second, hat2, scale2, norms[1])
    low2 = grad2.astype(BF)
    g_wco = mm_tn(cross, low2)
    grad_cross = mm_nt(low2, wco).astype(BF)
    grad_cq, enc_terms = cross_backward(cq, enc_kv, cross, grad_cross, cross_sum)
    grad_ekv = lax.psum_scatter(enc_terms, ("fsdp", "seq"), scatter_dimension=0, tiled=True)
    g_wckv = mm_tn(enc_in[0], grad_ekv)
    grad_enc = mm_nt(grad_ekv, wckv)
    g_wcq = mm_tn(first_low, grad_cq)
    grad_first = grad2 + mm_nt(grad_cq, wcq)
    grad1, gain1, bias1 = norm_back(grad_first, hat1, scale1, norms[0])
    low1 = grad1.astype(BF)
    g_wo = jnp.concatenate([mm_tn(att_rows[0], low1), mm_tn(att_rows[1], low1)], 0)
    g_norms = jnp.stack([gain1, gain2, gain3, bias1, bias2, bias3], 1)
    g_norms = jnp.pad(g_norms, ((0, 0), (0, 122)))
    g_mixed = reduce_rows(jnp.concatenate([g_wo, g_wcq, g_wco, g_wckv, g_norms], 1))
    grad_att = jnp.stack([mm_nt(low1, wo[:hg]), mm_nt(low1, wo[hg:])], 0).astype(BF)
    grad_att = exchange(grad_att)
    grad_joined, grad_pkv = self_backward(
        joined, prompt_kv, reach, place, conts, att, grad_att, sums
    )
    g_wq = lax.dot_general(
        x_all, grad_joined, (((0, 1), (0, 1)), ((), ())), preferred_element_type=F32
    )
    g_wkv = mm_tn(prompt_all, grad_pkv)
    g_wq = g_wq + jnp.pad(g_wkv, ((0, 0), (hg, 0)))
    part = lax.psum_scatter(g_wq.astype(BF), "fsdp", scatter_dimension=0, tiled=True)
    part = (part.astype(F32) + swap(part, "grp").astype(F32)).astype(BF)
    q_low, q_high = both_halves(part)
    g_qkv = jnp.stack([q_low.reshape(shard, 3, hg), q_high.reshape(shard, 3, hg)], 2)
    g_qkv = g_qkv.reshape(shard, 3 * width).astype(F32)
    grad_x = lax.dot_general(
        grad_joined, wq, (((2,), (1,)), ((), ())), preferred_element_type=F32
    ).astype(BF)
    grad_x = exchange(grad_x)
    grad_in = grad1 + grad_x[0].astype(F32) + grad_x[1].astype(F32)
    grad_pr = lax.psum_scatter(
        mm_nt(grad_pkv, wq[:, hg:]).astype(BF), ("fsdp", "seq"), scatter_dimension=0, tiled=True
    )
    grad_prompt = grad_in[rows_c:] + grad_pr.astype(F32)

    g_norms = g_mixed[:, 5 * width :]
    return (
        third[rows_c:][None],
        third[:rows_c].reshape(cont_in.shape),
        grad_prompt[None],
        grad_in[:rows_c].reshape(cont_in.shape),
        grad_enc[None],
        g_qkv,
        g_mixed[:, :width],
        g_mixed[:, width : 2 * width],
        g_mixed[:, 3 * width : 5 * width],
        g_mixed[:, 2 * width : 3 * width],
        g_w1,
        g_w2,
        g_norms[:, :3].T,
        g_norms[:, 3:6].T,
    )


def solution(mesh):
    rows = P("grp", ("fsdp", "seq"), None)
    conts = P("grp", "fsdp", "seq", None)
    weight = P("fsdp", None)
    norm = P(None, "fsdp")
    return jax.shard_map(
        on_device,
        mesh=mesh,
        in_specs=(rows, conts, rows, P("grp", "fsdp"), rows, conts) + (weight,) * 7 + (norm,) * 2,
        out_specs=(rows, conts, rows, conts, rows) + (weight,) * 7 + (norm,) * 2,
        check_vma=False,
    )
```

```python
import functools

import jax
import jax.numpy as jnp
from jax import lax
from jax.experimental import pallas as pl
from jax.experimental.pallas import tpu as pltpu
from jax.sharding import PartitionSpec as P

HEAD_DIM = 64
SCALE = 0.125
EPS = 1e-05
MASKED = -1e30
BF = jnp.bfloat16
F32 = jnp.float32


def mm(a, b):
    return jnp.dot(a, b, preferred_element_type=F32)


def mm_tn(a, b):
    return lax.dot_general(a, b, (((0,), (0,)), ((), ())), preferred_element_type=F32)


def mm_nt(a, b):
    return lax.dot_general(a, b, (((1,), (1,)), ((), ())), preferred_element_type=F32)


def swap(value, axis):
    return lax.ppermute(value, axis, [(0, 1), (1, 0)])


def half_rows(value):
    half = value.shape[0] // 2
    return lax.dynamic_slice_in_dim(value, lax.axis_index("seq") * half, half, 0)


def gather_rows(shard):
    return lax.all_gather(half_rows(shard), ("fsdp", "seq"), axis=0, tiled=True)


def both_halves(mine):
    other = swap(mine, "seq")
    first = lax.axis_index("seq") == 0
    low = jnp.where(first, mine, other)
    high = jnp.where(first, other, mine)
    return low, high


def scatter_sum(value):
    return lax.psum_scatter(value, ("fsdp", "seq"), scatter_dimension=0, tiled=True)


def per_owner(values):
    owners = 2 * lax.axis_size("fsdp")
    width = values[0].shape[-1]
    pieces = [v.reshape(owners, -1, width) for v in values]
    return jnp.concatenate(pieces, 1).reshape(-1, width)


def over_groups(part):
    return (part.astype(F32) + swap(part, "grp").astype(F32)).astype(BF)


def norm_stats(resid):
    average = jnp.mean(resid, axis=-1, keepdims=True)
    centred = resid - average
    variance = jnp.mean(centred * centred, axis=-1, keepdims=True)
    scale = lax.rsqrt(variance + EPS)
    return centred * scale, scale


def norm_back(grad, hat, scale, gain):
    weighted = grad * gain
    first = jnp.mean(weighted, axis=-1, keepdims=True)
    second = jnp.mean(weighted * hat, axis=-1, keepdims=True)
    back = scale * (weighted - first - hat * second)
    return back, jnp.sum(grad * hat, axis=0), jnp.sum(grad, axis=0)


def dot_nn(a, b):
    return lax.dot_general(a, b, (((1,), (0,)), ((), ())), preferred_element_type=F32)


def dot_nt(a, b):
    return lax.dot_general(a, b, (((1,), (1,)), ((), ())), preferred_element_type=F32)


def lane_masks():
    lane = lax.broadcasted_iota(jnp.int32, (1, 2 * HEAD_DIM), 1)
    low = lane < HEAD_DIM
    return low, jnp.where(low, 1.0, 0.0).astype(BF), jnp.where(low, 0.0, 1.0).astype(BF)


def forward_block(queries, segments):
    low, *masks = lane_masks()
    scaled = queries * BF(SCALE)
    outs, sums = [], []
    for mask in masks:
        own = scaled * mask
        scores = []
        for keys, _, hide in segments:
            part = dot_nt(own, keys)
            scores.append(part if hide is None else hide(part, 1))
        top = scores[0].max(axis=-1, keepdims=True)
        for part in scores[1:]:
            top = jnp.maximum(top, part.max(axis=-1, keepdims=True))
        total, out = 0.0, 0.0
        for part, (_, values, _) in zip(scores, segments):
            raised = jnp.exp(part - top)
            total = total + raised.sum(axis=-1, keepdims=True)
            out = out + dot_nn(raised.astype(BF), values)
        outs.append(out / total)
        sums.append(top + jnp.log(total))
    out = jnp.where(low, outs[0], outs[1]).astype(BF)
    return out, jnp.where(low, sums[0], sums[1])


def backward_block(queries, grad, out, log_sum, segments):
    _, *masks = lane_masks()
    scaled = queries * BF(SCALE)
    delta = (grad.astype(F32) * out.astype(F32)).T
    owns = [scaled * mask for mask in masks]
    grads = [grad * mask for mask in masks]
    own_pair = jnp.concatenate(owns, 0)
    grad_pair = jnp.concatenate(grads, 0)
    grad_q = [0.0, 0.0]
    grad_kv = []
    for keys, turned, values, hide in segments:
        probs, slopes = [], []
        for h in range(2):
            span = slice(h * HEAD_DIM, (h + 1) * HEAD_DIM)
            scores = dot_nt(keys, owns[h])
            if hide is not None:
                scores = hide(scores, 0)
            prob = jnp.exp(scores - log_sum[h : h + 1])
            grad_prob = dot_nt(values, grads[h])
            slope = prob * (grad_prob - delta[span].sum(axis=0, keepdims=True))
            slope = slope.astype(BF)
            grad_q[h] = grad_q[h] + dot_nn(turned[span], slope)
            probs.append(prob.astype(BF))
            slopes.append(slope)
        grad_kv.append(
            (
                dot_nn(jnp.concatenate(slopes, 1), own_pair),
                dot_nn(jnp.concatenate(probs, 1), grad_pair),
            )
        )
    grad_q = jnp.concatenate(grad_q, 0).T * SCALE
    return grad_q.astype(BF), grad_kv


def hide_after(limit):
    def hide(scores, axis):
        key = lax.broadcasted_iota(jnp.int32, scores.shape, axis)
        return jnp.where(key < limit, scores, MASKED)

    return hide


def hide_future(start):
    def hide(scores, axis):
        key = lax.broadcasted_iota(jnp.int32, scores.shape, axis)
        query = lax.broadcasted_iota(jnp.int32, scores.shape, 1 - axis)
        return jnp.where(key <= query + start, scores, MASKED)

    return hide


def store_sums(ref, log_sum):
    turned = log_sum.T
    ref[0, 0, 0:1, : turned.shape[1]] = turned[0:1]
    ref[0, 0, 1:2, : turned.shape[1]] = turned[HEAD_DIM : HEAD_DIM + 1]


def own_spans(pos, block, half):
    spans = []
    for j in range(pos + 1):
        spans.append((j * block // half, j * block % half, block, j == pos))
    merged = []
    for span in spans:
        if merged and not span[3] and merged[-1][0] == span[0]:
            last = merged.pop()
            span = (last[0], last[1], last[2] + span[2], False)
        merged.append(span)
    return merged


def self_forward_kernel(
    info, q_ref, k_ref, v_ref, pk_ref, pv_ref, out_ref, sum_ref, *, half, count, rows_p, block
):
    step = pl.program_id(1)
    per = 2 * half // block
    for pos in range(per):

        @pl.when((step < count * per) & (lax.rem(step, per) == pos))
        def _():
            c = lax.div(step, per)
            base = pl.multiple_of(c * half, half)
            segments = [(pk_ref[...], pv_ref[...], hide_after(info[c]))]
            for source, offset, size, last in own_spans(pos, block, half):
                rows = pl.ds(base + offset, size)
                segments.append(
                    (k_ref[source, rows, :], v_ref[source, rows, :], hide_future(0) if last else None)
                )
            rows = pl.ds(base + pos * block % half, block)
            source = pos * block // half
            out, log_sum = forward_block(q_ref[source, rows, :], segments)
            out_ref[source, rows, :] = out
            store_sums(sum_ref, log_sum)

    @pl.when(step == count * per)
    def _():
        rows = slice(count * half, count * half + rows_p)
        queries = jnp.concatenate([q_ref[0, rows, :], q_ref[1, rows, :]], 0)
        out, log_sum = forward_block(queries, [(pk_ref[...], pv_ref[...], hide_future(info[count]))])
        out_ref[0, rows, :] = out[:rows_p]
        out_ref[1, rows, :] = out[rows_p:]
        store_sums(sum_ref, log_sum)


def self_backward_kernel(
    info,
    q_ref,
    k_ref,
    v_ref,
    pk_ref,
    pv_ref,
    out_ref,
    grad_ref,
    sum_ref,
    joined_ref,
    prompt_ref,
    acc_pk,
    acc_pv,
    acc_k,
    acc_v,
    turned_p,
    turned,
    *,
    half,
    count,
    rows_p,
    block,
):
    step = pl.program_id(1)
    per = 2 * half // block

    @pl.when(step == 0)
    def _():
        acc_pk[...] = jnp.zeros_like(acc_pk)
        acc_pv[...] = jnp.zeros_like(acc_pv)
        turned_p[...] = pk_ref[...].T

    for pos in range(per):

        @pl.when((step < count * per) & (lax.rem(step, per) == pos))
        def _():
            c = lax.div(step, per)
            base = pl.multiple_of(c * half, half)
            if pos == 0:
                for source in range(2):
                    turned[:, source * half : (source + 1) * half] = k_ref[
                        source, pl.ds(base, half), :
                    ].T
            spans = own_spans(pos, block, half)
            segments = [(pk_ref[...], turned_p[...], pv_ref[...], hide_after(info[c]))]
            for source, offset, size, last in spans:
                rows = pl.ds(base + offset, size)
                at = source * half + offset
                segments.append(
                    (
                        k_ref[source, rows, :],
                        turned[:, at : at + size],
                        v_ref[source, rows, :],
                        hide_future(0) if last else None,
                    )
                )
            rows = pl.ds(base + pos * block % half, block)
            source = pos * block // half
            grad_q, grad_kv = backward_block(
                q_ref[source, rows, :],
                grad_ref[source, rows, :],
                out_ref[source, rows, :],
                sum_ref[0, 0],
                segments,
            )
            joined_ref[0, source, rows, :] = grad_q
            acc_pk[...] += grad_kv[0][0]
            acc_pv[...] += grad_kv[0][1]
            for (source, offset, size, last), (grad_k, grad_v) in zip(spans, grad_kv[1:]):
                at = source * half + offset
                if last:
                    acc_k[at : at + size] = grad_k
                    acc_v[at : at + size] = grad_v
                else:
                    acc_k[at : at + size] += grad_k
                    acc_v[at : at + size] += grad_v
            if pos == per - 1:
                for source in range(2):
                    rows = pl.ds(base, half)
                    span = slice(source * half, (source + 1) * half)
                    joined_ref[1, source, rows, :] = acc_k[span].astype(BF)
                    joined_ref[2, source, rows, :] = acc_v[span].astype(BF)

    @pl.when(step == count * per)
    def _():
        rows = slice(count * half, count * half + rows_p)
        both = [jnp.concatenate([r[0, rows, :], r[1, rows, :]], 0) for r in (q_ref, grad_ref, out_ref)]
        grad_q, grad_kv = backward_block(
            *both,
            sum_ref[0, 0][:, : 2 * rows_p],
            [(pk_ref[...], turned_p[...], pv_ref[...], hide_future(info[count]))],
        )
        for source in range(2):
            joined_ref[0, source, rows, :] = grad_q[source * rows_p : (source + 1) * rows_p]
            zero = jnp.zeros((rows_p, grad_q.shape[1]), BF)
            joined_ref[1, source, rows, :] = zero
            joined_ref[2, source, rows, :] = zero
        prompt_ref[0] = (acc_pk[...] + grad_kv[0][0]).astype(BF)
        prompt_ref[1] = (acc_pv[...] + grad_kv[0][1]).astype(BF)


PAIR = 2 * HEAD_DIM
BLOCK = 256


def wide(rows, at, lead=()):
    shape = lead + (rows, PAIR)
    zeros = (0,) * (len(lead) + 1)
    return pl.BlockSpec(shape, lambda pair, step, *_: zeros + (at + pair,))


def sums_spec(block):
    return pl.BlockSpec((1, 1, 8, block), lambda pair, step, *_: (pair, step, 0, 0))


def cost(flops, exps, *arrays):
    return pl.CostEstimate(
        flops=flops,
        transcendentals=exps,
        bytes_accessed=sum(a.size * a.dtype.itemsize for a in arrays),
    )


def self_forward(joined, prompt_kv, info, half, count, rows_p):
    rows, width = joined.shape[1], joined.shape[2] // 3
    keys = prompt_kv.shape[0]
    pairs = width // PAIR
    block = min(BLOCK, half)
    steps = count * 2 * half // block + 1
    scores = 2 * pairs * (count * 2 * half * (keys + half) + 2 * rows_p * keys)
    return pl.pallas_call(
        functools.partial(self_forward_kernel, half=half, count=count, rows_p=rows_p, block=block),
        out_shape=(
            jax.ShapeDtypeStruct((2, rows, width), BF),
            jax.ShapeDtypeStruct((pairs, steps, 8, block), F32),
        ),
        grid_spec=pltpu.PrefetchScalarGridSpec(
            num_scalar_prefetch=1,
            grid=(pairs, steps),
            in_specs=[
                wide(rows, 0, (2,)),
                wide(rows, pairs, (2,)),
                wide(rows, 2 * pairs, (2,)),
                wide(keys, 0),
                wide(keys, pairs),
            ],
            out_specs=[wide(rows, 0, (2,)), sums_spec(block)],
        ),
        cost_estimate=cost(scores * 512, scores, joined, prompt_kv),
        name="self_forward",
    )(info, joined, joined, joined, prompt_kv, prompt_kv)


def self_backward(joined, prompt_kv, info, out, grad, sums, half, count, rows_p):
    rows, width = joined.shape[1], joined.shape[2] // 3
    keys = prompt_kv.shape[0]
    pairs = width // PAIR
    block = min(BLOCK, half)
    steps = count * 2 * half // block + 1
    scores = 2 * pairs * (count * 2 * half * (keys + half) + 2 * rows_p * keys)
    return pl.pallas_call(
        functools.partial(self_backward_kernel, half=half, count=count, rows_p=rows_p, block=block),
        out_shape=(
            jax.ShapeDtypeStruct((3, 2, rows, width), BF),
            jax.ShapeDtypeStruct((2, keys, width), BF),
        ),
        grid_spec=pltpu.PrefetchScalarGridSpec(
            num_scalar_prefetch=1,
            grid=(pairs, steps),
            in_specs=[
                wide(rows, 0, (2,)),
                wide(rows, pairs, (2,)),
                wide(rows, 2 * pairs, (2,)),
                wide(keys, 0),
                wide(keys, pairs),
                wide(rows, 0, (2,)),
                wide(rows, 0, (2,)),
                sums_spec(block),
            ],
            out_specs=[wide(rows, 0, (3, 2)), wide(keys, 0, (2,))],
            scratch_shapes=[pltpu.VMEM((keys, PAIR), F32)] * 2
            + [pltpu.VMEM((2 * half, PAIR), F32)] * 2
            + [pltpu.VMEM((PAIR, keys), BF), pltpu.VMEM((PAIR, 2 * half), BF)],
        ),
        cost_estimate=cost(scores * 1280, scores, joined, prompt_kv, out, grad, joined),
        name="self_backward",
    )(info, joined, joined, joined, prompt_kv, prompt_kv, out, grad, sums)


def cross_forward_kernel(q_ref, k_ref, v_ref, out_ref, sum_ref, *, full, rest, block):
    step = pl.program_id(1)

    @pl.when(step < full)
    def _():
        rows = pl.ds(pl.multiple_of(step * block, block), block)
        out, log_sum = forward_block(q_ref[rows, :], [(k_ref[...], v_ref[...], None)])
        out_ref[rows, :] = out
        store_sums(sum_ref, log_sum)

    @pl.when(step == full)
    def _():
        rows = slice(full * block, full * block + rest)
        out, log_sum = forward_block(q_ref[rows, :], [(k_ref[...], v_ref[...], None)])
        out_ref[rows, :] = out
        store_sums(sum_ref, log_sum)


def cross_backward_kernel(
    q_ref, k_ref, v_ref, out_ref, grad_ref, sum_ref, gq_ref, gk_ref, gv_ref, acc_k, acc_v, turned, *, full, rest, block
):
    step = pl.program_id(1)

    @pl.when(step == 0)
    def _():
        acc_k[...] = jnp.zeros_like(acc_k)
        acc_v[...] = jnp.zeros_like(acc_v)
        turned[...] = k_ref[...].T

    def piece(rows, size):
        grad_q, grad_kv = backward_block(
            q_ref[rows, :],
            grad_ref[rows, :],
            out_ref[rows, :],
            sum_ref[0, 0][:, :size],
            [(k_ref[...], turned[...], v_ref[...], None)],
        )
        gq_ref[rows, :] = grad_q
        return grad_kv[0]

    @pl.when(step < full)
    def _():
        grad_k, grad_v = piece(pl.ds(pl.multiple_of(step * block, block), block), block)
        acc_k[...] += grad_k
        acc_v[...] += grad_v

    @pl.when(step == full)
    def _():
        grad_k, grad_v = piece(slice(full * block, full * block + rest), rest)
        gk_ref[...] = (acc_k[...] + grad_k).astype(BF)
        gv_ref[...] = (acc_v[...] + grad_v).astype(BF)


def cross_forward(queries, enc_kv, rows_c):
    rows, width = queries.shape
    keys = enc_kv.shape[0]
    pairs = width // PAIR
    full = rows_c // BLOCK
    scores = 2 * pairs * rows * keys
    return pl.pallas_call(
        functools.partial(cross_forward_kernel, full=full, rest=rows - rows_c, block=BLOCK),
        out_shape=(
            jax.ShapeDtypeStruct((rows, width), BF),
            jax.ShapeDtypeStruct((pairs, full + 1, 8, BLOCK), F32),
        ),
        grid=(pairs, full + 1),
        in_specs=[wide(rows, 0), wide(keys, 0), wide(keys, pairs)],
        out_specs=[wide(rows, 0), sums_spec(BLOCK)],
        cost_estimate=cost(scores * 512, scores, queries, enc_kv),
        name="cross_forward",
    )(queries, enc_kv, enc_kv)


def cross_backward(queries, enc_kv, out, grad, sums, rows_c):
    rows, width = queries.shape
    keys = enc_kv.shape[0]
    pairs = width // PAIR
    full = rows_c // BLOCK
    scores = 2 * pairs * rows * keys
    return pl.pallas_call(
        functools.partial(cross_backward_kernel, full=full, rest=rows - rows_c, block=BLOCK),
        out_shape=(
            jax.ShapeDtypeStruct((rows, width), BF),
            jax.ShapeDtypeStruct((keys, width), BF),
            jax.ShapeDtypeStruct((keys, width), BF),
        ),
        grid=(pairs, full + 1),
        in_specs=[
            wide(rows, 0),
            wide(keys, 0),
            wide(keys, pairs),
            wide(rows, 0),
            wide(rows, 0),
            sums_spec(BLOCK),
        ],
        out_specs=[wide(rows, 0), wide(keys, 0), wide(keys, 0)],
        scratch_shapes=[pltpu.VMEM((keys, PAIR), F32)] * 2 + [pltpu.VMEM((PAIR, keys), BF)],
        cost_estimate=cost(scores * 1280, scores, queries, enc_kv, out, grad),
        name="cross_backward",
    )(queries, enc_kv, enc_kv, out, grad, sums)


def exchange(value):
    return lax.all_to_all(value, "seq", split_axis=0, concat_axis=0, tiled=True)


def on_device(
    prompt_in,
    cont_in,
    enc_in,
    prefix,
    cot_prompt,
    cot_cont,
    w_qkv,
    w_attn_out,
    w_cross_q,
    w_cross_kv,
    w_cross_out,
    w_ffn_in,
    w_ffn_out,
    norm_gain,
    norm_bias,
):
    seq = lax.axis_index("seq")
    width = w_qkv.shape[1] // 3
    hg = width // 2
    shard = w_qkv.shape[0]
    rows_p = prompt_in.shape[1]
    count = cont_in.shape[1]
    half = cont_in.shape[2]
    rows_c = count * half
    reach = prefix[0]

    own_cols = lax.dynamic_slice_in_dim(w_qkv.reshape(shard, 3, 2, hg), seq, 1, 2)
    wq = lax.all_gather(own_cols.reshape(shard, 3 * hg), "fsdp", axis=0, tiled=True)
    shared = lax.all_gather(
        jnp.concatenate([prompt_in[0], enc_in[0]], 0), ("fsdp", "seq"), axis=0
    )
    prompt_all = shared[:, :rows_p].reshape(-1, width)
    enc_all = shared[:, rows_p:].reshape(-1, width)
    norms = jnp.concatenate([norm_gain, norm_bias], 0).T
    norms = jnp.pad(norms, ((0, 0), (0, 128 - norms.shape[1])))
    mixed = gather_rows(jnp.concatenate([w_attn_out, w_cross_q, w_cross_out, w_cross_kv, norms], 1))
    wo = mixed[:, :width]
    wcq = mixed[:, width : 2 * width]
    wco = mixed[:, 2 * width : 3 * width]
    wckv = mixed[:, 3 * width : 5 * width]
    norms = mixed[:, 5 * width :].astype(F32).T
    w1 = gather_rows(w_ffn_in)
    w2 = gather_rows(w_ffn_out)

    mine = jnp.concatenate([cont_in[0].reshape(rows_c, width), prompt_in[0]], 0)
    x_low, x_high = both_halves(mine)
    x_all = jnp.stack([x_low, x_high], 0)
    joined = lax.dot_general(
        x_all, wq, (((2,), (0,)), ((), ())), preferred_element_type=F32
    ).astype(BF)
    prompt_kv = mm(prompt_all, wq[:, hg:]).astype(BF)
    info = jnp.concatenate([reach, lax.axis_index("fsdp")[None] * (2 * rows_p)])
    att, sums = self_forward(joined, prompt_kv, info, half, count, rows_p)
    att_rows = exchange(att)
    proj = mm(att_rows[0], wo[:hg]) + mm(att_rows[1], wo[hg:])
    hat1, scale1 = norm_stats(mine.astype(F32) + proj)
    first = hat1 * norms[0] + norms[3]
    first_low = first.astype(BF)
    cq = mm(first_low, wcq).astype(BF)
    enc_kv = mm(enc_all, wckv).astype(BF)
    cross, cross_sum = cross_forward(cq, enc_kv, rows_c)
    hat2, scale2 = norm_stats(first + mm(cross, wco))
    second = hat2 * norms[1] + norms[4]
    second_low = second.astype(BF)
    pre = mm(second_low, w1)
    gate = 0.5 * (1.0 + lax.erf(pre * 0.7071067811865476))
    act = (pre * gate).astype(BF)
    slope = (gate + pre * jnp.exp(-0.5 * pre * pre) * 0.3989422804014327).astype(BF)
    hat3, scale3 = norm_stats(second + mm(act, w2))
    third = (hat3 * norms[2] + norms[5]).astype(BF)

    cot = jnp.concatenate([cot_cont[0].reshape(rows_c, width), cot_prompt[0]], 0).astype(F32)
    grad3, gain3, bias3 = norm_back(cot, hat3, scale3, norms[2])
    low3 = grad3.astype(BF)
    g_w2 = mm_tn(act, low3).astype(BF)
    grad_pre = (mm_nt(low3, w2) * slope.astype(F32)).astype(BF)
    g_w1 = mm_tn(second_low, grad_pre).astype(BF)
    owners = 2 * lax.axis_size("fsdp")
    columns = [slice(i, i + width) for i in range(0, g_w1.shape[1], width)]
    g_ffn = per_owner([g_w2] + [g_w1[:, cols] for cols in columns])
    grad_second = grad3 + mm_nt(grad_pre, w1)
    grad2, gain2, bias2 = norm_back(grad_second, hat2, scale2, norms[1])
    low2, g_ffn = lax.optimization_barrier((grad2.astype(BF), g_ffn))
    g_ffn = scatter_sum(g_ffn)
    g_wco = mm_tn(cross, low2)
    grad_cross = mm_nt(low2, wco).astype(BF)
    grad_cq, grad_ck, grad_cv = cross_backward(cq, enc_kv, cross, grad_cross, cross_sum, rows_c)
    g_wckv = [mm_tn(enc_all, grad_ck), mm_tn(enc_all, grad_cv)]
    grad_enc = (mm_nt(grad_ck, wckv[:, :width]) + mm_nt(grad_cv, wckv[:, width:])).astype(BF)
    g_wcq = mm_tn(first_low, grad_cq)
    grad_first = grad2 + mm_nt(grad_cq, wcq)
    grad1, gain1, bias1 = norm_back(grad_first, hat1, scale1, norms[0])
    low1 = grad1.astype(BF)
    g_wo = jnp.concatenate([mm_tn(att_rows[0], low1), mm_tn(att_rows[1], low1)], 0)
    g_norms = jnp.stack([gain1, gain2, gain3, bias1, bias2, bias3], 0).astype(BF)
    g_norms = g_norms.reshape(6, owners, shard // 2).swapaxes(0, 1)
    g_norms = jnp.pad(g_norms, ((0, 0), (0, 10), (0, width - shard // 2))).reshape(-1, width)
    g_mixed = [g.astype(BF) for g in (g_wo, g_wcq, g_wco, *g_wckv, grad_enc, g_norms)]
    g_mixed = per_owner(g_mixed)
    grad_att = jnp.stack([mm_nt(low1, wo[:hg]), mm_nt(low1, wo[hg:])], 0).astype(BF)
    grad_att, g_mixed, g_ffn = lax.optimization_barrier((exchange(grad_att), g_mixed, g_ffn))
    g_mixed = scatter_sum(g_mixed)
    grad_joined, grad_pkv = self_backward(
        joined, prompt_kv, info, att, grad_att, sums, half, count, rows_p
    )
    grad_joined, g_mixed = lax.optimization_barrier((grad_joined, g_mixed))
    flat = x_all.reshape(-1, width)
    g_q, g_k, g_v = (mm_tn(flat, grad_joined[i].reshape(-1, hg)) for i in range(3))
    g_k = g_k + mm_tn(prompt_all, grad_pkv[0])
    g_v = g_v + mm_tn(prompt_all, grad_pkv[1])
    grad_pr = mm_nt(grad_pkv[0], wq[:, hg : 2 * hg]) + mm_nt(grad_pkv[1], wq[:, 2 * hg :])
    chips = lax.axis_size("fsdp")
    last = [g_q, g_k, g_v, grad_pr[:, :hg], grad_pr[:, hg:]]
    last = jnp.concatenate([v.astype(BF).reshape(chips, -1, hg) for v in last], 1)
    last = lax.psum_scatter(
        last.reshape(-1, hg), "fsdp", scatter_dimension=0, tiled=True
    )
    q_low, q_high = both_halves(over_groups(last[: 3 * shard]))
    g_qkv = [v.reshape(3, shard, hg) for v in (q_low, q_high)]
    g_qkv = jnp.concatenate([g_qkv[i % 2][i // 2] for i in range(6)], 1).astype(F32)
    grad_x = sum(
        mm_nt(grad_joined[i].reshape(-1, hg), wq[:, i * hg : (i + 1) * hg]) for i in range(3)
    )
    grad_x = grad_x.astype(BF).reshape(x_all.shape)
    cont_x = exchange(grad_x[:, :rows_c])
    grad_in = grad1[:rows_c] + cont_x[0].astype(F32) + cont_x[1].astype(F32)
    grad_pr = last[3 * shard :].reshape(2, 2 * rows_p, hg)
    grad_pr = jnp.concatenate([grad_pr[0], grad_pr[1]], 1).reshape(2, rows_p, width)
    prompt_x = exchange((grad_x[:, rows_c:].astype(F32) + grad_pr.astype(F32)).astype(BF))
    grad_prompt = grad1[rows_c:] + prompt_x[0].astype(F32) + prompt_x[1].astype(F32)

    both = both_halves(over_groups(g_ffn))
    g_w2 = jnp.concatenate([v[: 2 * shard] for v in both], 0).astype(F32)
    mine = shard // 2
    g_w1 = [
        jnp.concatenate([v[2 * shard + i * mine :][:mine] for i in range(len(columns))], 1)
        for v in both
    ]
    g_w1 = jnp.concatenate(g_w1, 0).astype(F32)
    used = 5 * mine
    grad_enc = g_mixed[used : used + rows_p].astype(F32)
    g_mixed = jnp.concatenate([g_mixed[:used], g_mixed[used + rows_p :]], 0)
    both = both_halves(over_groups(g_mixed))
    g_wo, g_wcq, g_wco, g_wck, g_wcv = (
        jnp.concatenate([v[i * mine : (i + 1) * mine] for v in both], 0).astype(F32)
        for i in range(5)
    )
    g_norms = jnp.concatenate([v[used : used + 6, :mine] for v in both], 1).astype(F32)
    return (
        third[rows_c:][None],
        third[:rows_c].reshape(cont_in.shape),
        grad_prompt[None],
        grad_in.reshape(cont_in.shape),
        grad_enc[None],
        g_qkv,
        g_wo,
        g_wcq,
        jnp.concatenate([g_wck, g_wcv], 1),
        g_wco,
        g_w1,
        g_w2,
        g_norms[:3],
        g_norms[3:],
    )


def solution(mesh):
    rows = P("grp", ("fsdp", "seq"), None)
    conts = P("grp", "fsdp", "seq", None)
    weight = P("fsdp", None)
    norm = P(None, "fsdp")
    return jax.shard_map(
        on_device,
        mesh=mesh,
        in_specs=(rows, conts, rows, P("grp", "fsdp"), rows, conts) + (weight,) * 7 + (norm,) * 2,
        out_specs=(rows, conts, rows, conts, rows) + (weight,) * 7 + (norm,) * 2,
        check_vma=False,
    )
```

```python
import functools

import jax
import jax.numpy as jnp
from jax import lax
from jax.experimental import pallas as pl
from jax.experimental.pallas import tpu as pltpu
from jax.sharding import PartitionSpec as P

HEAD_DIM = 64
SCALE = 0.125
EPS = 1e-05
MASKED = -1e30
BF = jnp.bfloat16
PAIR = 2 * HEAD_DIM
FLAGS = object()
MESH = pl.DeviceIdType.MESH
F32 = jnp.float32


def mm(a, b):
    return jnp.dot(a, b, preferred_element_type=F32)


def mm_tn(a, b):
    return lax.dot_general(a, b, (((0,), (0,)), ((), ())), preferred_element_type=F32)


def mm_nt(a, b):
    return lax.dot_general(a, b, (((1,), (1,)), ((), ())), preferred_element_type=F32)


def swap(value, axis):
    return lax.ppermute(value, axis, [(0, 1), (1, 0)])


def half_rows(value):
    half = value.shape[0] // 2
    return lax.dynamic_slice_in_dim(value, lax.axis_index("seq") * half, half, 0)


def gather_rows(shard):
    return lax.all_gather(half_rows(shard), ("fsdp", "seq"), axis=0, tiled=True)


def both_halves(mine):
    other = swap(mine, "seq")
    first = lax.axis_index("seq") == 0
    low = jnp.where(first, mine, other)
    high = jnp.where(first, other, mine)
    return low, high


def scatter_sum(value):
    return lax.psum_scatter(value, ("fsdp", "seq"), scatter_dimension=0, tiled=True)


def per_owner(values):
    owners = 2 * lax.axis_size("fsdp")
    width = values[0].shape[-1]
    pieces = [v.reshape(owners, -1, width) for v in values]
    return jnp.concatenate(pieces, 1).reshape(-1, width)


def over_groups(part):
    return (part.astype(F32) + swap(part, "grp").astype(F32)).astype(BF)


def norm_stats(resid):
    average = jnp.mean(resid, axis=-1, keepdims=True)
    centred = resid - average
    variance = jnp.mean(centred * centred, axis=-1, keepdims=True)
    scale = lax.rsqrt(variance + EPS)
    return centred * scale, scale


def norm_back(grad, hat, scale, gain):
    weighted = grad * gain
    first = jnp.mean(weighted, axis=-1, keepdims=True)
    second = jnp.mean(weighted * hat, axis=-1, keepdims=True)
    back = scale * (weighted - first - hat * second)
    return back, jnp.sum(grad * hat, axis=0), jnp.sum(grad, axis=0)


def dot_nn(a, b):
    return lax.dot_general(a, b, (((1,), (0,)), ((), ())), preferred_element_type=F32)


def dot_nt(a, b):
    return lax.dot_general(a, b, (((1,), (1,)), ((), ())), preferred_element_type=F32)


def lane_masks():
    lane = lax.broadcasted_iota(jnp.int32, (1, 2 * HEAD_DIM), 1)
    low = lane < HEAD_DIM
    return low, jnp.where(low, 1.0, 0.0).astype(BF), jnp.where(low, 0.0, 1.0).astype(BF)


def with_flags(queries):
    lane = lax.broadcasted_iota(jnp.int32, (1, PAIR), 1)
    _, *masks = lane_masks()
    flags = [jnp.where(lane == at, 1.0, 0.0).astype(BF) for at in (HEAD_DIM, 0)]
    return [queries * mask + flag for mask, flag in zip(masks, flags)]


def flag_keys(flagged, keys, limit):
    lane = lax.broadcasted_iota(jnp.int32, keys.shape, 1)
    key = lax.broadcasted_iota(jnp.int32, keys.shape, 0)
    bias = jnp.where(key < limit, 0.0, MASKED)
    for h, at in enumerate((HEAD_DIM, 0)):
        flagged[h] = jnp.where(lane == at, bias, keys.astype(F32)).astype(BF)


def forward_block(queries, segments):
    low, *masks = lane_masks()
    scaled = queries * BF(SCALE)
    outs, sums = [], []
    flagged = with_flags(scaled)
    for h, mask in enumerate(masks):
        own = scaled * mask
        scores = []
        for keys, _, hide in segments:
            part = dot_nt(flagged[h], keys[h]) if hide is FLAGS else dot_nt(own, keys)
            hide = None if hide is FLAGS else hide
            scores.append(part if hide is None else hide(part, 1))
        top = scores[0].max(axis=-1, keepdims=True)
        for part in scores[1:]:
            top = jnp.maximum(top, part.max(axis=-1, keepdims=True))
        total, out = 0.0, 0.0
        for part, (_, values, _) in zip(scores, segments):
            raised = jnp.exp(part - top)
            total = total + raised.sum(axis=-1, keepdims=True)
            out = out + dot_nn(raised.astype(BF), values)
        outs.append(out / total)
        sums.append(top + jnp.log(total))
    out = jnp.where(low, outs[0], outs[1]).astype(BF)
    return out, jnp.where(low, sums[0], sums[1])


def backward_block(queries, grad, out, log_sum, segments):
    _, *masks = lane_masks()
    scaled = queries * BF(SCALE)
    delta = (grad.astype(F32) * out.astype(F32)).T
    owns = [scaled * mask for mask in masks]
    grads = [grad * mask for mask in masks]
    own_pair = jnp.concatenate(owns, 0)
    flagged = with_flags(scaled)
    grad_pair = jnp.concatenate(grads, 0)
    grad_q = [0.0, 0.0]
    grad_kv = []
    for keys, turned, values, hide in segments:
        probs, slopes = [], []
        for h in range(2):
            span = slice(h * HEAD_DIM, (h + 1) * HEAD_DIM)
            scores = dot_nt(keys[h], flagged[h]) if hide is FLAGS else dot_nt(keys, owns[h])
            if hide is not None and hide is not FLAGS:
                scores = hide(scores, 0)
            prob = jnp.exp(scores - log_sum[h : h + 1])
            grad_prob = dot_nt(values, grads[h])
            slope = prob * (grad_prob - delta[span].sum(axis=0, keepdims=True))
            slope = slope.astype(BF)
            grad_q[h] = grad_q[h] + dot_nn(turned[span], slope)
            probs.append(prob.astype(BF))
            slopes.append(slope)
        grad_kv.append(
            (
                dot_nn(jnp.concatenate(slopes, 1), own_pair),
                dot_nn(jnp.concatenate(probs, 1), grad_pair),
            )
        )
    grad_q = jnp.concatenate(grad_q, 0).T * SCALE
    return grad_q.astype(BF), grad_kv


def hide_future(start):
    def hide(scores, axis):
        key = lax.broadcasted_iota(jnp.int32, scores.shape, axis)
        query = lax.broadcasted_iota(jnp.int32, scores.shape, 1 - axis)
        return jnp.where(key <= query + start, scores, MASKED)

    return hide


def store_sums(ref, log_sum):
    turned = log_sum.T
    ref[0, 0, 0:1, : turned.shape[1]] = turned[0:1]
    ref[0, 0, 1:2, : turned.shape[1]] = turned[HEAD_DIM : HEAD_DIM + 1]


def own_spans(pos, block, half):
    spans = []
    for j in range(pos + 1):
        spans.append((j * block // half, j * block % half, block, j == pos))
    merged = []
    for span in spans:
        if merged and not span[3] and merged[-1][0] == span[0]:
            last = merged.pop()
            span = (last[0], last[1], last[2] + span[2], False)
        merged.append(span)
    return merged


def self_forward_kernel(
    info, q_ref, k_ref, v_ref, pk_ref, pv_ref, out_ref, sum_ref, flagged, *, half, count, rows_p, block
):
    step = pl.program_id(1)
    per = 2 * half // block
    for pos in range(per):

        @pl.when((step < count * per) & (lax.rem(step, per) == pos))
        def _():
            c = lax.div(step, per)
            base = pl.multiple_of(c * half, half)
            if pos == 0:
                flag_keys(flagged, pk_ref[...], info[c])
            segments = [((flagged[0], flagged[1]), pv_ref[...], FLAGS)]
            for source, offset, size, last in own_spans(pos, block, half):
                rows = pl.ds(base + offset, size)
                segments.append(
                    (k_ref[source, rows, :], v_ref[source, rows, :], hide_future(0) if last else None)
                )
            rows = pl.ds(base + pos * block % half, block)
            source = pos * block // half
            out, log_sum = forward_block(q_ref[source, rows, :], segments)
            out_ref[source, rows, :] = out
            store_sums(sum_ref, log_sum)

    @pl.when(step == count * per)
    def _():
        rows = slice(count * half, count * half + rows_p)
        queries = jnp.concatenate([q_ref[0, rows, :], q_ref[1, rows, :]], 0)
        out, log_sum = forward_block(queries, [(pk_ref[...], pv_ref[...], hide_future(info[count]))])
        out_ref[0, rows, :] = out[:rows_p]
        out_ref[1, rows, :] = out[rows_p:]
        store_sums(sum_ref, log_sum)


def self_backward_kernel(
    info,
    q_ref,
    k_ref,
    v_ref,
    pk_ref,
    pv_ref,
    out_ref,
    grad_ref,
    sum_ref,
    joined_ref,
    prompt_ref,
    acc_pk,
    acc_pv,
    acc_k,
    acc_v,
    turned_p,
    turned,
    flagged,
    *,
    half,
    count,
    rows_p,
    block,
):
    step = pl.program_id(1)
    per = 2 * half // block

    @pl.when(step == 0)
    def _():
        acc_pk[...] = jnp.zeros_like(acc_pk)
        acc_pv[...] = jnp.zeros_like(acc_pv)
        turned_p[...] = pk_ref[...].T

    for pos in range(per):

        @pl.when((step < count * per) & (lax.rem(step, per) == pos))
        def _():
            c = lax.div(step, per)
            base = pl.multiple_of(c * half, half)
            if pos == 0:
                flag_keys(flagged, pk_ref[...], info[c])
                for source in range(2):
                    turned[:, source * half : (source + 1) * half] = k_ref[
                        source, pl.ds(base, half), :
                    ].T
            spans = own_spans(pos, block, half)
            segments = [((flagged[0], flagged[1]), turned_p[...], pv_ref[...], FLAGS)]
            for source, offset, size, last in spans:
                rows = pl.ds(base + offset, size)
                at = source * half + offset
                segments.append(
                    (
                        k_ref[source, rows, :],
                        turned[:, at : at + size],
                        v_ref[source, rows, :],
                        hide_future(0) if last else None,
                    )
                )
            rows = pl.ds(base + pos * block % half, block)
            source = pos * block // half
            grad_q, grad_kv = backward_block(
                q_ref[source, rows, :],
                grad_ref[source, rows, :],
                out_ref[source, rows, :],
                sum_ref[0, 0],
                segments,
            )
            joined_ref[0, source, rows, :] = grad_q
            acc_pk[...] += grad_kv[0][0]
            acc_pv[...] += grad_kv[0][1]
            for (source, offset, size, last), (grad_k, grad_v) in zip(spans, grad_kv[1:]):
                at = source * half + offset
                if last:
                    acc_k[at : at + size] = grad_k
                    acc_v[at : at + size] = grad_v
                else:
                    acc_k[at : at + size] += grad_k
                    acc_v[at : at + size] += grad_v
            if pos == per - 1:
                for source in range(2):
                    rows = pl.ds(base, half)
                    span = slice(source * half, (source + 1) * half)
                    joined_ref[1, source, rows, :] = acc_k[span].astype(BF)
                    joined_ref[2, source, rows, :] = acc_v[span].astype(BF)

    @pl.when(step == count * per)
    def _():
        rows = slice(count * half, count * half + rows_p)
        both = [jnp.concatenate([r[0, rows, :], r[1, rows, :]], 0) for r in (q_ref, grad_ref, out_ref)]
        grad_q, grad_kv = backward_block(
            *both,
            sum_ref[0, 0][:, : 2 * rows_p],
            [(pk_ref[...], turned_p[...], pv_ref[...], hide_future(info[count]))],
        )
        for source in range(2):
            joined_ref[0, source, rows, :] = grad_q[source * rows_p : (source + 1) * rows_p]
            zero = jnp.zeros((rows_p, grad_q.shape[1]), BF)
            joined_ref[1, source, rows, :] = zero
            joined_ref[2, source, rows, :] = zero
        prompt_ref[0] = (acc_pk[...] + grad_kv[0][0]).astype(BF)
        prompt_ref[1] = (acc_pv[...] + grad_kv[0][1]).astype(BF)


BLOCK = 512


def wide(rows, at, lead=()):
    shape = lead + (rows, PAIR)
    zeros = (0,) * (len(lead) + 1)
    return pl.BlockSpec(shape, lambda pair, step, *_: zeros + (at + pair,))


def sums_spec(block):
    return pl.BlockSpec((1, 1, 8, block), lambda pair, step, *_: (pair, step, 0, 0))


def cost(flops, exps, *arrays):
    return pl.CostEstimate(
        flops=flops,
        transcendentals=exps,
        bytes_accessed=sum(a.size * a.dtype.itemsize for a in arrays),
    )


def self_forward(joined, prompt_kv, info, half, count, rows_p):
    rows, width = joined[0].shape[1:]
    keys = prompt_kv[0].shape[0]
    pairs = width // PAIR
    block = min(BLOCK, half)
    steps = count * 2 * half // block + 1
    scores = 2 * pairs * (count * 2 * half * (keys + half) + 2 * rows_p * keys)
    return pl.pallas_call(
        functools.partial(self_forward_kernel, half=half, count=count, rows_p=rows_p, block=block),
        out_shape=(
            jax.ShapeDtypeStruct((2, rows, width), BF),
            jax.ShapeDtypeStruct((pairs, steps, 8, block), F32),
        ),
        grid_spec=pltpu.PrefetchScalarGridSpec(
            num_scalar_prefetch=1,
            grid=(pairs, steps),
            in_specs=[
                wide(rows, 0, (2,)),
                wide(rows, 0, (2,)),
                wide(rows, 0, (2,)),
                wide(keys, 0),
                wide(keys, 0),
            ],
            out_specs=[wide(rows, 0, (2,)), sums_spec(block)],
            scratch_shapes=[pltpu.VMEM((2, keys, PAIR), BF)],
        ),
        cost_estimate=cost(scores * 512, scores, *joined, *prompt_kv),
        name="self_forward",
    )(info, *joined, *prompt_kv)


def self_backward(joined, prompt_kv, info, out, grad, sums, half, count, rows_p):
    rows, width = joined[0].shape[1:]
    keys = prompt_kv[0].shape[0]
    pairs = width // PAIR
    block = min(BLOCK, half)
    steps = count * 2 * half // block + 1
    scores = 2 * pairs * (count * 2 * half * (keys + half) + 2 * rows_p * keys)
    return pl.pallas_call(
        functools.partial(self_backward_kernel, half=half, count=count, rows_p=rows_p, block=block),
        out_shape=(
            jax.ShapeDtypeStruct((3, 2, rows, width), BF),
            jax.ShapeDtypeStruct((2, keys, width), BF),
        ),
        grid_spec=pltpu.PrefetchScalarGridSpec(
            num_scalar_prefetch=1,
            grid=(pairs, steps),
            in_specs=[
                wide(rows, 0, (2,)),
                wide(rows, 0, (2,)),
                wide(rows, 0, (2,)),
                wide(keys, 0),
                wide(keys, 0),
                wide(rows, 0, (2,)),
                wide(rows, 0, (2,)),
                sums_spec(block),
            ],
            out_specs=[wide(rows, 0, (3, 2)), wide(keys, 0, (2,))],
            scratch_shapes=[pltpu.VMEM((keys, PAIR), F32)] * 2
            + [pltpu.VMEM((2 * half, PAIR), F32)] * 2
            + [pltpu.VMEM((PAIR, keys), BF), pltpu.VMEM((PAIR, 2 * half), BF)]
            + [pltpu.VMEM((2, keys, PAIR), BF)],
        ),
        cost_estimate=cost(scores * 1280, scores, *joined, *prompt_kv, out, grad, *joined),
        name="self_backward",
    )(info, *joined, *prompt_kv, out, grad, sums)


def cross_forward_kernel(q_ref, k_ref, v_ref, out_ref, sum_ref, *, full, rest, block):
    step = pl.program_id(1)

    @pl.when(step < full)
    def _():
        rows = pl.ds(pl.multiple_of(step * block, block), block)
        out, log_sum = forward_block(q_ref[rows, :], [(k_ref[...], v_ref[...], None)])
        out_ref[rows, :] = out
        store_sums(sum_ref, log_sum)

    @pl.when(step == full)
    def _():
        rows = slice(full * block, full * block + rest)
        out, log_sum = forward_block(q_ref[rows, :], [(k_ref[...], v_ref[...], None)])
        out_ref[rows, :] = out
        store_sums(sum_ref, log_sum)


def cross_backward_kernel(
    q_ref, k_ref, v_ref, out_ref, grad_ref, sum_ref, gq_ref, gk_ref, gv_ref, acc_k, acc_v, turned, *, full, rest, block
):
    step = pl.program_id(1)

    @pl.when(step == 0)
    def _():
        acc_k[...] = jnp.zeros_like(acc_k)
        acc_v[...] = jnp.zeros_like(acc_v)
        turned[...] = k_ref[...].T

    def piece(rows, size):
        grad_q, grad_kv = backward_block(
            q_ref[rows, :],
            grad_ref[rows, :],
            out_ref[rows, :],
            sum_ref[0, 0][:, :size],
            [(k_ref[...], turned[...], v_ref[...], None)],
        )
        gq_ref[rows, :] = grad_q
        return grad_kv[0]

    @pl.when(step < full)
    def _():
        grad_k, grad_v = piece(pl.ds(pl.multiple_of(step * block, block), block), block)
        acc_k[...] += grad_k
        acc_v[...] += grad_v

    @pl.when(step == full)
    def _():
        grad_k, grad_v = piece(slice(full * block, full * block + rest), rest)
        gk_ref[...] = (acc_k[...] + grad_k).astype(BF)
        gv_ref[...] = (acc_v[...] + grad_v).astype(BF)


def cross_forward(queries, enc_kv, rows_c):
    rows, width = queries.shape
    keys = enc_kv.shape[0]
    pairs = width // PAIR
    full = rows_c // BLOCK
    scores = 2 * pairs * rows * keys
    return pl.pallas_call(
        functools.partial(cross_forward_kernel, full=full, rest=rows - rows_c, block=BLOCK),
        out_shape=(
            jax.ShapeDtypeStruct((rows, width), BF),
            jax.ShapeDtypeStruct((pairs, full + 1, 8, BLOCK), F32),
        ),
        grid=(pairs, full + 1),
        in_specs=[wide(rows, 0), wide(keys, 0), wide(keys, pairs)],
        out_specs=[wide(rows, 0), sums_spec(BLOCK)],
        cost_estimate=cost(scores * 512, scores, queries, enc_kv),
        name="cross_forward",
    )(queries, enc_kv, enc_kv)


def cross_backward(queries, enc_kv, out, grad, sums, rows_c):
    rows, width = queries.shape
    keys = enc_kv.shape[0]
    pairs = width // PAIR
    full = rows_c // BLOCK
    scores = 2 * pairs * rows * keys
    return pl.pallas_call(
        functools.partial(cross_backward_kernel, full=full, rest=rows - rows_c, block=BLOCK),
        out_shape=(
            jax.ShapeDtypeStruct((rows, width), BF),
            jax.ShapeDtypeStruct((keys, width), BF),
            jax.ShapeDtypeStruct((keys, width), BF),
        ),
        grid=(pairs, full + 1),
        in_specs=[
            wide(rows, 0),
            wide(keys, 0),
            wide(keys, pairs),
            wide(rows, 0),
            wide(rows, 0),
            sums_spec(BLOCK),
        ],
        out_specs=[wide(rows, 0), wide(keys, 0), wide(keys, 0)],
        scratch_shapes=[pltpu.VMEM((keys, PAIR), F32)] * 2 + [pltpu.VMEM((PAIR, keys), BF)],
        cost_estimate=cost(scores * 1280, scores, queries, enc_kv, out, grad),
        name="cross_backward",
    )(queries, enc_kv, enc_kv, out, grad, sums)


def line_events(count):
    return [None] + [(d, k) for k in range(count - 1) for d in (0, 1)]


def gather_kernel(
    w_ref, s_ref, c_ref, p_ref, w_out, s_out, x_out, own, x_sem, z_send, z_recv, p_send, p_recv, c_send, c_recv
):
    f, seq = lax.axis_index("fsdp"), lax.axis_index("seq")
    count = w_out.shape[1] // 2
    high, low = lax.div(f, 2), lax.rem(f, 2)
    pair = {"fsdp": f + 1 - 2 * low}
    core = {"seq": 1 - seq}
    signs = (1, -1)

    def inside(place):
        return (place >= 0) & (place < count)

    barrier = pltpu.get_barrier_semaphore()
    for where in (pair, core):
        pl.semaphore_signal(barrier, inc=1, device_id=where, device_id_type=MESH)
    for sign in signs:

        @pl.when(inside(high + sign))
        def _():
            pl.semaphore_signal(
                barrier, inc=1, device_id={"fsdp": f + 2 * sign}, device_id_type=MESH
            )

    edges = jnp.where(high > 0, 1, 0) + jnp.where(high < count - 1, 1, 0)
    pl.semaphore_wait(barrier, 2 + edges)

    def remote(src, dst, send, recv, where):
        return pltpu.make_async_remote_copy(
            src_ref=src, dst_ref=dst, send_sem=send, recv_sem=recv, device_id=where, device_id_type=MESH
        )

    rows_c = c_ref.shape[0]
    rows_p = p_ref.shape[0]
    places = [x_out.at[seq, pl.ds(0, rows_c)], x_out.at[seq, pl.ds(rows_c, rows_p)]]
    across = [
        remote(src, dst, x_sem.at[0, i], x_sem.at[1, i], core)
        for i, (src, dst) in enumerate(zip((c_ref, p_ref), places))
    ]
    local = [
        pltpu.make_async_copy(w_ref, w_out.at[:, f], own.at[0]),
        pltpu.make_async_copy(s_ref, s_out.at[:, f, seq], own.at[1]),
        pltpu.make_async_copy(c_ref, places[0], own.at[2]),
        pltpu.make_async_copy(p_ref, places[1], own.at[3]),
    ]

    def block(origin, side, first):
        index = 2 * origin + side
        held = (w_out.at[:, index], s_out.at[:, index, seq])
        return held, ((w_ref, s_ref) if first else held)

    def line_copies(d, k):
        held, source = block(high - signs[d] * k, low, k == 0)
        where = {"fsdp": f + 2 * signs[d]}
        return [
            remote(src, dst, z_send.at[d, k, i], z_recv.at[d, k, i], where)
            for i, (src, dst) in enumerate(zip(source, held))
        ]

    def pair_copies(event, origin, first):
        held, source = block(origin, low, first)
        return [
            remote(src, dst, p_send.at[event, i], p_recv.at[event, i], pair)
            for i, (src, dst) in enumerate(zip(source, held))
        ]

    def core_copy(event, origin, side, first):
        held, source = block(origin, side, first)
        return remote(source[1], held[1], c_send.at[event], c_recv.at[event], core)

    events = line_events(count)

    def origin_of(event):
        return high if event is None else high - signs[event[0]] * (event[1] + 1)

    def sends_on(d, k):
        return inside(high - signs[d] * k) & inside(high + signs[d])

    def gets(event):
        d, k = event
        return inside(high - signs[d]) & inside(high - signs[d] * (k + 1))

    def start_line(d, k):
        @pl.when(sends_on(d, k))
        def _():
            for copy in line_copies(d, k):
                copy.start()

    for d in (0, 1):
        start_line(d, 0)
    for copy in pair_copies(0, high, True):
        copy.start()
    for copy in across:
        copy.start()
    core_copy(0, high, low, True).start()
    for copy in local:
        copy.start()
    for number, event in enumerate(events[1:], 1):
        d, k = event

        @pl.when(gets(event))
        def _():
            origin = origin_of(event)
            held, _ = block(origin, low, False)
            for i, ref in enumerate(held):
                remote(ref, ref, z_send.at[d, k, i], z_recv.at[d, k, i], pair).wait_recv()
            if k + 1 < count - 1:

                @pl.when(inside(high + signs[d]))
                def _():
                    for copy in line_copies(d, k + 1):
                        copy.start()

            for copy in pair_copies(number, origin, False):
                copy.start()
            core_copy(number, origin, low, False).start()

    def finish(number, event):
        origin = origin_of(event)
        held, _ = block(origin, 1 - low, False)
        for i, ref in enumerate(held):
            remote(ref, ref, p_send.at[number, i], p_recv.at[number, i], pair).wait_recv()
        core_copy(len(events) + number, origin, 1 - low, False).start()

    def drain(number, event):
        origin = origin_of(event)
        for copy in pair_copies(number, origin, event is None):
            copy.wait_send()
        for place, side in ((number, low), (len(events) + number, 1 - low)):
            copy = core_copy(place, origin, side, event is None and side is low)
            copy.wait_send()
            theirs = s_out.at[:, 2 * origin + side, 1 - seq]
            remote(theirs, theirs, c_send.at[place], c_recv.at[place], core).wait_recv()

    for act in (finish, drain):
        for number, event in enumerate(events):
            if event is None:
                act(number, event)
            else:
                pl.when(gets(event))(functools.partial(act, number, event))
    for d in (0, 1):
        for k in range(count - 1):

            @pl.when(sends_on(d, k))
            def _():
                for copy in line_copies(d, k):
                    copy.wait_send()

    for i, copy in enumerate(across):
        copy.wait_send()
        theirs = x_out.at[1 - seq, pl.ds(0, rows_c) if i == 0 else pl.ds(rows_c, rows_p)]
        remote(theirs, theirs, x_sem.at[0, i], x_sem.at[1, i], core).wait_recv()
    for copy in local:
        copy.wait()


def gather_start(w_own, s_own, cont_rows, prompt_rows):
    chips = lax.axis_size("fsdp")
    count = chips // 2
    events = len(line_events(count))
    rows = cont_rows.shape[0] + prompt_rows.shape[0]
    dma = pltpu.SemaphoreType.DMA
    vmem = pl.BlockSpec(memory_space=pltpu.VMEM)
    kinds, depth, width = w_own.shape
    return pl.pallas_call(
        gather_kernel,
        out_shape=(
            jax.ShapeDtypeStruct((kinds, chips, depth, width), BF),
            jax.ShapeDtypeStruct((2, chips, 2) + s_own.shape[1:], BF),
            jax.ShapeDtypeStruct((2, rows, cont_rows.shape[1]), BF),
        ),
        in_specs=[vmem] * 4,
        out_specs=[vmem] * 3,
        scratch_shapes=[
            dma((4,)),
            dma((2, 2)),
            dma((2, count - 1, 2)),
            dma((2, count - 1, 2)),
            dma((events, 2)),
            dma((events, 2)),
            dma((2 * events,)),
            dma((2 * events,)),
        ],
        compiler_params=pltpu.CompilerParams(collective_id=0, has_side_effects=True),
        name="gather_start",
    )(w_own, s_own, cont_rows, prompt_rows)


def exchange(value):
    return lax.all_to_all(value, "seq", split_axis=0, concat_axis=0, tiled=True)


def on_device(
    prompt_in,
    cont_in,
    enc_in,
    prefix,
    cot_prompt,
    cot_cont,
    w_qkv,
    w_attn_out,
    w_cross_q,
    w_cross_kv,
    w_cross_out,
    w_ffn_in,
    w_ffn_out,
    norm_gain,
    norm_bias,
):
    seq = lax.axis_index("seq")
    width = w_qkv.shape[1] // 3
    hg = width // 2
    shard = w_qkv.shape[0]
    rows_p = prompt_in.shape[1]
    count = cont_in.shape[1]
    half = cont_in.shape[2]
    rows_c = count * half
    reach = prefix[0]

    own = lax.dynamic_index_in_dim(w_qkv.reshape(shard, 3, 2, hg), seq, 2, False).swapaxes(0, 1)
    pair = jnp.stack([prompt_in[0], enc_in[0]], 0)
    wq, shared, x_all = gather_start(own, pair, cont_in[0].reshape(rows_c, width), prompt_in[0])
    wq = wq.reshape(3, -1, hg)
    prompt_all = shared[0].reshape(-1, width)
    enc_all = shared[1].reshape(-1, width)
    norms = jnp.concatenate([norm_gain, norm_bias], 0).T
    norms = jnp.pad(norms, ((0, 0), (0, 128 - norms.shape[1])))
    mixed = jnp.concatenate([w_attn_out, w_cross_q, w_cross_out, w_cross_kv, norms], 1)
    mixed, x_all = lax.optimization_barrier((mixed, x_all))
    mixed = gather_rows(mixed)
    wo = mixed[:, :width]
    wcq = mixed[:, width : 2 * width]
    wco = mixed[:, 2 * width : 3 * width]
    wckv = mixed[:, 3 * width : 5 * width]
    norms = mixed[:, 5 * width :].astype(F32).T
    w_ffn_in, w_ffn_out, x_all = lax.optimization_barrier((w_ffn_in, w_ffn_out, x_all))
    w1 = gather_rows(w_ffn_in)
    w2 = gather_rows(w_ffn_out)

    mine = jnp.concatenate([cont_in[0].reshape(rows_c, width), prompt_in[0]], 0)
    flat = x_all.reshape(-1, width)
    joined = tuple(mm(flat, w).astype(BF).reshape(2, -1, hg) for w in wq)
    prompt_kv = (mm(prompt_all, wq[1]).astype(BF), mm(prompt_all, wq[2]).astype(BF))
    info = jnp.concatenate([reach, lax.axis_index("fsdp")[None] * (2 * rows_p)])
    att, sums = self_forward(joined, prompt_kv, info, half, count, rows_p)
    att_rows = exchange(att)
    proj = mm(att_rows[0], wo[:hg]) + mm(att_rows[1], wo[hg:])
    hat1, scale1 = norm_stats(mine.astype(F32) + proj)
    first = hat1 * norms[0] + norms[3]
    first_low = first.astype(BF)
    cq = mm(first_low, wcq).astype(BF)
    enc_kv = mm(enc_all, wckv).astype(BF)
    cross, cross_sum = cross_forward(cq, enc_kv, rows_c)
    hat2, scale2 = norm_stats(first + mm(cross, wco))
    second = hat2 * norms[1] + norms[4]
    second_low = second.astype(BF)
    pre = mm(second_low, w1)
    gate = 0.5 * (1.0 + lax.erf(pre * 0.7071067811865476))
    act = (pre * gate).astype(BF)
    slope = (gate + pre * jnp.exp(-0.5 * pre * pre) * 0.3989422804014327).astype(BF)
    hat3, scale3 = norm_stats(second + mm(act, w2))
    third = (hat3 * norms[2] + norms[5]).astype(BF)

    cot = jnp.concatenate([cot_cont[0].reshape(rows_c, width), cot_prompt[0]], 0).astype(F32)
    grad3, gain3, bias3 = norm_back(cot, hat3, scale3, norms[2])
    low3 = grad3.astype(BF)
    g_w2 = mm_tn(act, low3).astype(BF)
    grad_pre = (mm_nt(low3, w2) * slope.astype(F32)).astype(BF)
    g_w1 = mm_tn(second_low, grad_pre).astype(BF)
    owners = 2 * lax.axis_size("fsdp")
    columns = [slice(i, i + width) for i in range(0, g_w1.shape[1], width)]
    g_ffn = per_owner([g_w2] + [g_w1[:, cols] for cols in columns])
    grad_second = grad3 + mm_nt(grad_pre, w1)
    grad2, gain2, bias2 = norm_back(grad_second, hat2, scale2, norms[1])
    low2, g_ffn = lax.optimization_barrier((grad2.astype(BF), g_ffn))
    g_ffn = scatter_sum(g_ffn)
    g_wco = mm_tn(cross, low2)
    grad_cross = mm_nt(low2, wco).astype(BF)
    grad_cq, grad_ck, grad_cv = cross_backward(cq, enc_kv, cross, grad_cross, cross_sum, rows_c)
    g_wckv = [mm_tn(enc_all, grad_ck), mm_tn(enc_all, grad_cv)]
    grad_enc = (mm_nt(grad_ck, wckv[:, :width]) + mm_nt(grad_cv, wckv[:, width:])).astype(BF)
    g_wcq = mm_tn(first_low, grad_cq)
    grad_first = grad2 + mm_nt(grad_cq, wcq)
    grad1, gain1, bias1 = norm_back(grad_first, hat1, scale1, norms[0])
    low1 = grad1.astype(BF)
    g_wo = jnp.concatenate([mm_tn(att_rows[0], low1), mm_tn(att_rows[1], low1)], 0)
    g_norms = jnp.stack([gain1, gain2, gain3, bias1, bias2, bias3], 0).astype(BF)
    g_norms = g_norms.reshape(6, owners, shard // 2).swapaxes(0, 1)
    g_norms = jnp.pad(g_norms, ((0, 0), (0, 10), (0, width - shard // 2))).reshape(-1, width)
    g_mixed = [g.astype(BF) for g in (g_wo, g_wcq, g_wco, *g_wckv, grad_enc, g_norms)]
    g_mixed = per_owner(g_mixed)
    grad_att = jnp.stack([mm_nt(low1, wo[:hg]), mm_nt(low1, wo[hg:])], 0).astype(BF)
    grad_att, g_mixed, g_ffn = lax.optimization_barrier((exchange(grad_att), g_mixed, g_ffn))
    g_mixed = scatter_sum(g_mixed)
    grad_joined, grad_pkv = self_backward(
        joined, prompt_kv, info, att, grad_att, sums, half, count, rows_p
    )
    g_q, g_k, g_v = (mm_tn(flat, grad_joined[i].reshape(-1, hg)) for i in range(3))
    g_k = g_k + mm_tn(prompt_all, grad_pkv[0])
    g_v = g_v + mm_tn(prompt_all, grad_pkv[1])
    grad_pr = mm_nt(grad_pkv[0], wq[1]) + mm_nt(grad_pkv[1], wq[2])
    chips = lax.axis_size("fsdp")
    last = [g_q, g_k, g_v, grad_pr[:, :hg], grad_pr[:, hg:]]
    last = jnp.concatenate([v.astype(BF).reshape(chips, -1, hg) for v in last], 1)
    last, g_mixed = lax.optimization_barrier((last.reshape(-1, hg), g_mixed))
    last = lax.psum_scatter(last, "fsdp", scatter_dimension=0, tiled=True)
    q_low, q_high = both_halves(over_groups(last[: 3 * shard]))
    g_qkv = [v.reshape(3, shard, hg) for v in (q_low, q_high)]
    g_qkv = jnp.concatenate([g_qkv[i % 2][i // 2] for i in range(6)], 1).astype(F32)
    grad_x = sum(
        mm_nt(grad_joined[i].reshape(-1, hg), wq[i]) for i in range(3)
    )
    grad_x = grad_x.astype(BF).reshape(x_all.shape)
    cont_x = exchange(grad_x[:, :rows_c])
    grad_in = grad1[:rows_c] + cont_x[0].astype(F32) + cont_x[1].astype(F32)
    grad_pr = last[3 * shard :].reshape(2, 2 * rows_p, hg)
    grad_pr = jnp.concatenate([grad_pr[0], grad_pr[1]], 1).reshape(2, rows_p, width)
    prompt_x = exchange((grad_x[:, rows_c:].astype(F32) + grad_pr.astype(F32)).astype(BF))
    grad_prompt = grad1[rows_c:] + prompt_x[0].astype(F32) + prompt_x[1].astype(F32)

    both = both_halves(over_groups(g_ffn))
    g_w2 = jnp.concatenate([v[: 2 * shard] for v in both], 0).astype(F32)
    mine = shard // 2
    g_w1 = [
        jnp.concatenate([v[2 * shard + i * mine :][:mine] for i in range(len(columns))], 1)
        for v in both
    ]
    g_w1 = jnp.concatenate(g_w1, 0).astype(F32)
    used = 5 * mine
    grad_enc = g_mixed[used : used + rows_p].astype(F32)
    g_mixed = jnp.concatenate([g_mixed[:used], g_mixed[used + rows_p :]], 0)
    both = both_halves(over_groups(g_mixed))
    g_wo, g_wcq, g_wco, g_wck, g_wcv = (
        jnp.concatenate([v[i * mine : (i + 1) * mine] for v in both], 0).astype(F32)
        for i in range(5)
    )
    g_norms = jnp.concatenate([v[used : used + 6, :mine] for v in both], 1).astype(F32)
    return (
        third[rows_c:][None],
        third[:rows_c].reshape(cont_in.shape),
        grad_prompt[None],
        grad_in.reshape(cont_in.shape),
        grad_enc[None],
        g_qkv,
        g_wo,
        g_wcq,
        jnp.concatenate([g_wck, g_wcv], 1),
        g_wco,
        g_w1,
        g_w2,
        g_norms[:3],
        g_norms[3:],
    )


def solution(mesh):
    rows = P("grp", ("fsdp", "seq"), None)
    conts = P("grp", "fsdp", "seq", None)
    weight = P("fsdp", None)
    norm = P(None, "fsdp")
    return jax.shard_map(
        on_device,
        mesh=mesh,
        in_specs=(rows, conts, rows, P("grp", "fsdp"), rows, conts) + (weight,) * 7 + (norm,) * 2,
        out_specs=(rows, conts, rows, conts, rows) + (weight,) * 7 + (norm,) * 2,
        check_vma=False,
    )
```

```python
import functools

import jax
import jax.numpy as jnp
from jax import lax
from jax.experimental import pallas as pl
from jax.experimental.pallas import tpu as pltpu
from jax.sharding import PartitionSpec as P

HEAD_DIM = 64
SCALE = 0.125
EPS = 1e-05
MASKED = -1e30
BF = jnp.bfloat16
PAIR = 2 * HEAD_DIM
FLAGS = object()
MESH = pl.DeviceIdType.MESH
F32 = jnp.float32


def mm(a, b):
    return jnp.dot(a, b, preferred_element_type=F32)


def mm_tn(a, b):
    return lax.dot_general(a, b, (((0,), (0,)), ((), ())), preferred_element_type=F32)


def mm_nt(a, b):
    return lax.dot_general(a, b, (((1,), (1,)), ((), ())), preferred_element_type=F32)


def swap(value, axis):
    return lax.ppermute(value, axis, [(0, 1), (1, 0)])


def half_rows(value):
    half = value.shape[0] // 2
    return lax.dynamic_slice_in_dim(value, lax.axis_index("seq") * half, half, 0)


def gather_rows(shard):
    return lax.all_gather(half_rows(shard), ("fsdp", "seq"), axis=0, tiled=True)


def scatter_sum(value):
    return lax.psum_scatter(value, ("fsdp", "seq"), scatter_dimension=0, tiled=True)


def per_owner(values):
    owners = 2 * lax.axis_size("fsdp")
    width = values[0].shape[-1]
    pieces = [v.reshape(owners, -1, width) for v in values]
    return jnp.concatenate(pieces, 1).reshape(-1, width)


def total_halves(part):
    across = [(i, 3 - i) for i in range(4)]
    terms = (part, swap(part, "grp")), (swap(part, "seq"), lax.ppermute(part, ("grp", "seq"), across))
    mine, other = ((a.astype(F32) + b.astype(F32)).astype(BF) for a, b in terms)
    first = lax.axis_index("seq") == 0
    return jnp.where(first, mine, other), jnp.where(first, other, mine)


def norm_stats(resid):
    average = jnp.mean(resid, axis=-1, keepdims=True)
    centred = resid - average
    variance = jnp.mean(centred * centred, axis=-1, keepdims=True)
    scale = lax.rsqrt(variance + EPS)
    return centred * scale, scale


def norm_back(grad, hat, scale, gain):
    weighted = grad * gain
    first = jnp.mean(weighted, axis=-1, keepdims=True)
    second = jnp.mean(weighted * hat, axis=-1, keepdims=True)
    back = scale * (weighted - first - hat * second)
    return back, jnp.sum(grad * hat, axis=0), jnp.sum(grad, axis=0)


def dot_nn(a, b):
    return lax.dot_general(a, b, (((1,), (0,)), ((), ())), preferred_element_type=F32)


def dot_nt(a, b):
    return lax.dot_general(a, b, (((1,), (1,)), ((), ())), preferred_element_type=F32)


def lane_masks():
    lane = lax.broadcasted_iota(jnp.int32, (1, 2 * HEAD_DIM), 1)
    low = lane < HEAD_DIM
    return low, jnp.where(low, 1.0, 0.0).astype(BF), jnp.where(low, 0.0, 1.0).astype(BF)


def with_flags(queries):
    lane = lax.broadcasted_iota(jnp.int32, (1, PAIR), 1)
    _, *masks = lane_masks()
    flags = [jnp.where(lane == at, 1.0, 0.0).astype(BF) for at in (HEAD_DIM, 0)]
    return [queries * mask + flag for mask, flag in zip(masks, flags)]


def flag_keys(flagged, keys, limit):
    lane = lax.broadcasted_iota(jnp.int32, keys.shape, 1)
    key = lax.broadcasted_iota(jnp.int32, keys.shape, 0)
    bias = jnp.where(key < limit, 0.0, MASKED)
    for h, at in enumerate((HEAD_DIM, 0)):
        flagged[h] = jnp.where(lane == at, bias, keys.astype(F32)).astype(BF)


def forward_block(queries, segments):
    low, *masks = lane_masks()
    scaled = queries * BF(SCALE)
    outs, sums = [], []
    flagged = with_flags(scaled)
    for h, mask in enumerate(masks):
        own = scaled * mask
        scores = []
        for keys, _, hide in segments:
            part = dot_nt(flagged[h], keys[h]) if hide is FLAGS else dot_nt(own, keys)
            hide = None if hide is FLAGS else hide
            scores.append(part if hide is None else hide(part, 1))
        top = scores[0].max(axis=-1, keepdims=True)
        for part in scores[1:]:
            top = jnp.maximum(top, part.max(axis=-1, keepdims=True))
        total, out = 0.0, 0.0
        for part, (_, values, _) in zip(scores, segments):
            raised = jnp.exp(part - top)
            total = total + raised.sum(axis=-1, keepdims=True)
            out = out + dot_nn(raised.astype(BF), values)
        outs.append(out / total)
        sums.append(top + jnp.log(total))
    out = jnp.where(low, outs[0], outs[1]).astype(BF)
    return out, jnp.where(low, sums[0], sums[1])


def backward_block(queries, grad, out, log_sum, segments):
    _, *masks = lane_masks()
    scaled = queries * BF(SCALE)
    delta = (grad.astype(F32) * out.astype(F32)).T
    owns = [scaled * mask for mask in masks]
    grads = [grad * mask for mask in masks]
    own_pair = jnp.concatenate(owns, 0)
    flagged = with_flags(scaled)
    grad_pair = jnp.concatenate(grads, 0)
    grad_q = [0.0, 0.0]
    grad_kv = []
    for keys, turned, values, hide in segments:
        probs, slopes = [], []
        for h in range(2):
            span = slice(h * HEAD_DIM, (h + 1) * HEAD_DIM)
            scores = dot_nt(keys[h], flagged[h]) if hide is FLAGS else dot_nt(keys, owns[h])
            if hide is not None and hide is not FLAGS:
                scores = hide(scores, 0)
            prob = jnp.exp(scores - log_sum[h : h + 1])
            grad_prob = dot_nt(values, grads[h])
            slope = prob * (grad_prob - delta[span].sum(axis=0, keepdims=True))
            slope = slope.astype(BF)
            grad_q[h] = grad_q[h] + dot_nn(turned[span], slope)
            probs.append(prob.astype(BF))
            slopes.append(slope)
        grad_kv.append(
            (
                dot_nn(jnp.concatenate(slopes, 1), own_pair),
                dot_nn(jnp.concatenate(probs, 1), grad_pair),
            )
        )
    grad_q = jnp.concatenate(grad_q, 0).T * SCALE
    return grad_q.astype(BF), grad_kv


def hide_future(start):
    def hide(scores, axis):
        key = lax.broadcasted_iota(jnp.int32, scores.shape, axis)
        query = lax.broadcasted_iota(jnp.int32, scores.shape, 1 - axis)
        return jnp.where(key <= query + start, scores, MASKED)

    return hide


def store_sums(ref, log_sum):
    turned = log_sum.T
    ref[0, 0, 0:1, : turned.shape[1]] = turned[0:1]
    ref[0, 0, 1:2, : turned.shape[1]] = turned[HEAD_DIM : HEAD_DIM + 1]


def own_spans(pos, block, half):
    spans = []
    for j in range(pos + 1):
        spans.append((j * block // half, j * block % half, block, j == pos))
    merged = []
    for span in spans:
        if merged and not span[3] and merged[-1][0] == span[0]:
            last = merged.pop()
            span = (last[0], last[1], last[2] + span[2], False)
        merged.append(span)
    return merged


def self_forward_kernel(
    info, q_ref, k_ref, v_ref, pk_ref, pv_ref, out_ref, sum_ref, flagged, *, half, count, rows_p, block
):
    step = pl.program_id(1)
    per = 2 * half // block
    for pos in range(per):

        @pl.when((step < count * per) & (lax.rem(step, per) == pos))
        def _():
            c = lax.div(step, per)
            base = pl.multiple_of(c * half, half)
            if pos == 0:
                flag_keys(flagged, pk_ref[...], info[c])
            segments = [((flagged[0], flagged[1]), pv_ref[...], FLAGS)]
            for source, offset, size, last in own_spans(pos, block, half):
                rows = pl.ds(base + offset, size)
                segments.append(
                    (k_ref[source, rows, :], v_ref[source, rows, :], hide_future(0) if last else None)
                )
            rows = pl.ds(base + pos * block % half, block)
            source = pos * block // half
            out, log_sum = forward_block(q_ref[source, rows, :], segments)
            out_ref[source, rows, :] = out
            store_sums(sum_ref, log_sum)

    @pl.when(step == count * per)
    def _():
        rows = slice(count * half, count * half + rows_p)
        queries = jnp.concatenate([q_ref[0, rows, :], q_ref[1, rows, :]], 0)
        out, log_sum = forward_block(queries, [(pk_ref[...], pv_ref[...], hide_future(info[count]))])
        out_ref[0, rows, :] = out[:rows_p]
        out_ref[1, rows, :] = out[rows_p:]
        store_sums(sum_ref, log_sum)


def self_backward_kernel(
    info,
    q_ref,
    k_ref,
    v_ref,
    pk_ref,
    pv_ref,
    out_ref,
    grad_ref,
    sum_ref,
    joined_ref,
    prompt_ref,
    acc_pk,
    acc_pv,
    acc_k,
    acc_v,
    turned_p,
    turned,
    flagged,
    *,
    half,
    count,
    rows_p,
    block,
):
    step = pl.program_id(1)
    per = 2 * half // block

    @pl.when(step == 0)
    def _():
        acc_pk[...] = jnp.zeros_like(acc_pk)
        acc_pv[...] = jnp.zeros_like(acc_pv)
        turned_p[...] = pk_ref[...].T

    for pos in range(per):

        @pl.when((step < count * per) & (lax.rem(step, per) == pos))
        def _():
            c = lax.div(step, per)
            base = pl.multiple_of(c * half, half)
            if pos == 0:
                flag_keys(flagged, pk_ref[...], info[c])
                for source in range(2):
                    turned[:, source * half : (source + 1) * half] = k_ref[
                        source, pl.ds(base, half), :
                    ].T
            spans = own_spans(pos, block, half)
            segments = [((flagged[0], flagged[1]), turned_p[...], pv_ref[...], FLAGS)]
            for source, offset, size, last in spans:
                rows = pl.ds(base + offset, size)
                at = source * half + offset
                segments.append(
                    (
                        k_ref[source, rows, :],
                        turned[:, at : at + size],
                        v_ref[source, rows, :],
                        hide_future(0) if last else None,
                    )
                )
            rows = pl.ds(base + pos * block % half, block)
            source = pos * block // half
            grad_q, grad_kv = backward_block(
                q_ref[source, rows, :],
                grad_ref[source, rows, :],
                out_ref[source, rows, :],
                sum_ref[0, 0],
                segments,
            )
            joined_ref[0, source, rows, :] = grad_q
            acc_pk[...] += grad_kv[0][0]
            acc_pv[...] += grad_kv[0][1]
            for (source, offset, size, last), (grad_k, grad_v) in zip(spans, grad_kv[1:]):
                at = source * half + offset
                if last:
                    acc_k[at : at + size] = grad_k
                    acc_v[at : at + size] = grad_v
                else:
                    acc_k[at : at + size] += grad_k
                    acc_v[at : at + size] += grad_v
            if pos == per - 1:
                for source in range(2):
                    rows = pl.ds(base, half)
                    span = slice(source * half, (source + 1) * half)
                    joined_ref[1, source, rows, :] = acc_k[span].astype(BF)
                    joined_ref[2, source, rows, :] = acc_v[span].astype(BF)

    @pl.when(step == count * per)
    def _():
        rows = slice(count * half, count * half + rows_p)
        both = [jnp.concatenate([r[0, rows, :], r[1, rows, :]], 0) for r in (q_ref, grad_ref, out_ref)]
        grad_q, grad_kv = backward_block(
            *both,
            sum_ref[0, 0][:, : 2 * rows_p],
            [(pk_ref[...], turned_p[...], pv_ref[...], hide_future(info[count]))],
        )
        for source in range(2):
            joined_ref[0, source, rows, :] = grad_q[source * rows_p : (source + 1) * rows_p]
            zero = jnp.zeros((rows_p, grad_q.shape[1]), BF)
            joined_ref[1, source, rows, :] = zero
            joined_ref[2, source, rows, :] = zero
        prompt_ref[0] = (acc_pk[...] + grad_kv[0][0]).astype(BF)
        prompt_ref[1] = (acc_pv[...] + grad_kv[0][1]).astype(BF)


BLOCK = 512


def wide(rows, at, lead=()):
    shape = lead + (rows, PAIR)
    zeros = (0,) * (len(lead) + 1)
    return pl.BlockSpec(shape, lambda pair, step, *_: zeros + (at + pair,))


def sums_spec(block):
    return pl.BlockSpec((1, 1, 8, block), lambda pair, step, *_: (pair, step, 0, 0))


def cost(flops, exps, *arrays):
    return pl.CostEstimate(
        flops=flops,
        transcendentals=exps,
        bytes_accessed=sum(a.size * a.dtype.itemsize for a in arrays),
    )


def self_forward(joined, prompt_kv, info, half, count, rows_p):
    rows, width = joined[0].shape[1:]
    keys = prompt_kv[0].shape[0]
    pairs = width // PAIR
    block = min(BLOCK, half)
    steps = count * 2 * half // block + 1
    scores = 2 * pairs * (count * 2 * half * (keys + half) + 2 * rows_p * keys)
    return pl.pallas_call(
        functools.partial(self_forward_kernel, half=half, count=count, rows_p=rows_p, block=block),
        out_shape=(
            jax.ShapeDtypeStruct((2, rows, width), BF),
            jax.ShapeDtypeStruct((pairs, steps, 8, block), F32),
        ),
        grid_spec=pltpu.PrefetchScalarGridSpec(
            num_scalar_prefetch=1,
            grid=(pairs, steps),
            in_specs=[
                wide(rows, 0, (2,)),
                wide(rows, 0, (2,)),
                wide(rows, 0, (2,)),
                wide(keys, 0),
                wide(keys, 0),
            ],
            out_specs=[wide(rows, 0, (2,)), sums_spec(block)],
            scratch_shapes=[pltpu.VMEM((2, keys, PAIR), BF)],
        ),
        cost_estimate=cost(scores * 512, scores, *joined, *prompt_kv),
        name="self_forward",
    )(info, *joined, *prompt_kv)


def self_backward(joined, prompt_kv, info, out, grad, sums, half, count, rows_p):
    rows, width = joined[0].shape[1:]
    keys = prompt_kv[0].shape[0]
    pairs = width // PAIR
    block = min(BLOCK, half)
    steps = count * 2 * half // block + 1
    scores = 2 * pairs * (count * 2 * half * (keys + half) + 2 * rows_p * keys)
    return pl.pallas_call(
        functools.partial(self_backward_kernel, half=half, count=count, rows_p=rows_p, block=block),
        out_shape=(
            jax.ShapeDtypeStruct((3, 2, rows, width), BF),
            jax.ShapeDtypeStruct((2, keys, width), BF),
        ),
        grid_spec=pltpu.PrefetchScalarGridSpec(
            num_scalar_prefetch=1,
            grid=(pairs, steps),
            in_specs=[
                wide(rows, 0, (2,)),
                wide(rows, 0, (2,)),
                wide(rows, 0, (2,)),
                wide(keys, 0),
                wide(keys, 0),
                wide(rows, 0, (2,)),
                wide(rows, 0, (2,)),
                sums_spec(block),
            ],
            out_specs=[wide(rows, 0, (3, 2)), wide(keys, 0, (2,))],
            scratch_shapes=[pltpu.VMEM((keys, PAIR), F32)] * 2
            + [pltpu.VMEM((2 * half, PAIR), F32)] * 2
            + [pltpu.VMEM((PAIR, keys), BF), pltpu.VMEM((PAIR, 2 * half), BF)]
            + [pltpu.VMEM((2, keys, PAIR), BF)],
        ),
        cost_estimate=cost(scores * 1280, scores, *joined, *prompt_kv, out, grad, *joined),
        name="self_backward",
    )(info, *joined, *prompt_kv, out, grad, sums)


def cross_forward_kernel(q_ref, k_ref, v_ref, out_ref, sum_ref, *, full, rest, block):
    step = pl.program_id(1)

    @pl.when(step < full)
    def _():
        rows = pl.ds(pl.multiple_of(step * block, block), block)
        out, log_sum = forward_block(q_ref[rows, :], [(k_ref[...], v_ref[...], None)])
        out_ref[rows, :] = out
        store_sums(sum_ref, log_sum)

    @pl.when(step == full)
    def _():
        rows = slice(full * block, full * block + rest)
        out, log_sum = forward_block(q_ref[rows, :], [(k_ref[...], v_ref[...], None)])
        out_ref[rows, :] = out
        store_sums(sum_ref, log_sum)


def cross_backward_kernel(
    q_ref, k_ref, v_ref, out_ref, grad_ref, sum_ref, gq_ref, gk_ref, gv_ref, acc_k, acc_v, turned, *, full, rest, block
):
    step = pl.program_id(1)

    @pl.when(step == 0)
    def _():
        acc_k[...] = jnp.zeros_like(acc_k)
        acc_v[...] = jnp.zeros_like(acc_v)
        turned[...] = k_ref[...].T

    def piece(rows, size):
        grad_q, grad_kv = backward_block(
            q_ref[rows, :],
            grad_ref[rows, :],
            out_ref[rows, :],
            sum_ref[0, 0][:, :size],
            [(k_ref[...], turned[...], v_ref[...], None)],
        )
        gq_ref[rows, :] = grad_q
        return grad_kv[0]

    @pl.when(step < full)
    def _():
        grad_k, grad_v = piece(pl.ds(pl.multiple_of(step * block, block), block), block)
        acc_k[...] += grad_k
        acc_v[...] += grad_v

    @pl.when(step == full)
    def _():
        grad_k, grad_v = piece(slice(full * block, full * block + rest), rest)
        gk_ref[...] = (acc_k[...] + grad_k).astype(BF)
        gv_ref[...] = (acc_v[...] + grad_v).astype(BF)


def cross_forward(queries, enc_kv, rows_c):
    rows, width = queries.shape
    keys = enc_kv.shape[0]
    pairs = width // PAIR
    full = rows_c // BLOCK
    scores = 2 * pairs * rows * keys
    return pl.pallas_call(
        functools.partial(cross_forward_kernel, full=full, rest=rows - rows_c, block=BLOCK),
        out_shape=(
            jax.ShapeDtypeStruct((rows, width), BF),
            jax.ShapeDtypeStruct((pairs, full + 1, 8, BLOCK), F32),
        ),
        grid=(pairs, full + 1),
        in_specs=[wide(rows, 0), wide(keys, 0), wide(keys, pairs)],
        out_specs=[wide(rows, 0), sums_spec(BLOCK)],
        cost_estimate=cost(scores * 512, scores, queries, enc_kv),
        name="cross_forward",
    )(queries, enc_kv, enc_kv)


def cross_backward(queries, enc_kv, out, grad, sums, rows_c):
    rows, width = queries.shape
    keys = enc_kv.shape[0]
    pairs = width // PAIR
    full = rows_c // BLOCK
    scores = 2 * pairs * rows * keys
    return pl.pallas_call(
        functools.partial(cross_backward_kernel, full=full, rest=rows - rows_c, block=BLOCK),
        out_shape=(
            jax.ShapeDtypeStruct((rows, width), BF),
            jax.ShapeDtypeStruct((keys, width), BF),
            jax.ShapeDtypeStruct((keys, width), BF),
        ),
        grid=(pairs, full + 1),
        in_specs=[
            wide(rows, 0),
            wide(keys, 0),
            wide(keys, pairs),
            wide(rows, 0),
            wide(rows, 0),
            sums_spec(BLOCK),
        ],
        out_specs=[wide(rows, 0), wide(keys, 0), wide(keys, 0)],
        scratch_shapes=[pltpu.VMEM((keys, PAIR), F32)] * 2 + [pltpu.VMEM((PAIR, keys), BF)],
        cost_estimate=cost(scores * 1280, scores, queries, enc_kv, out, grad),
        name="cross_backward",
    )(queries, enc_kv, enc_kv, out, grad, sums)


def line_events(count):
    return [None] + [(d, k) for k in range(count - 1) for d in (0, 1)]


def gather_kernel(
    w_ref, s_ref, c_ref, p_ref, w_out, s_out, x_out, own, x_sem, z_send, z_recv, p_send, p_recv, g_send, g_recv, c_send, c_recv
):
    f, seq = lax.axis_index("fsdp"), lax.axis_index("seq")
    count = w_out.shape[1] // 2
    high, low = lax.div(f, 2), lax.rem(f, 2)
    pair = {"fsdp": f + 1 - 2 * low}
    core = {"seq": 1 - seq}
    group = lax.axis_index("grp")
    twin = {"grp": 1 - group}
    signs = (1, -1)

    def inside(place):
        return (place >= 0) & (place < count)

    barrier = pltpu.get_barrier_semaphore()
    for where in (pair, core, twin):
        pl.semaphore_signal(barrier, inc=1, device_id=where, device_id_type=MESH)
    for sign in signs:

        @pl.when(inside(high + sign))
        def _():
            pl.semaphore_signal(
                barrier, inc=1, device_id={"fsdp": f + 2 * sign}, device_id_type=MESH
            )

    edges = jnp.where(high > 0, 1, 0) + jnp.where(high < count - 1, 1, 0)
    pl.semaphore_wait(barrier, 3 + edges)

    def remote(src, dst, send, recv, where):
        return pltpu.make_async_remote_copy(
            src_ref=src, dst_ref=dst, send_sem=send, recv_sem=recv, device_id=where, device_id_type=MESH
        )

    rows_c = c_ref.shape[0]
    rows_p = p_ref.shape[0]
    places = [x_out.at[seq, pl.ds(0, rows_c)], x_out.at[seq, pl.ds(rows_c, rows_p)]]
    across = [
        remote(src, dst, x_sem.at[0, i], x_sem.at[1, i], core)
        for i, (src, dst) in enumerate(zip((c_ref, p_ref), places))
    ]
    local = [
        pltpu.make_async_copy(w_ref, w_out.at[:, f], own.at[0]),
        pltpu.make_async_copy(s_ref, s_out.at[:, f, seq], own.at[1]),
        pltpu.make_async_copy(c_ref, places[0], own.at[2]),
        pltpu.make_async_copy(p_ref, places[1], own.at[3]),
    ]

    def block(origin, side, first):
        index = 2 * origin + side
        held = (w_out.at[:, index], s_out.at[:, index, seq])
        return held, ((w_ref, s_ref) if first else held)

    def line_copies(d, k):
        held, source = block(high - signs[d] * k, low, k == 0)
        where = {"fsdp": f + 2 * signs[d]}
        return [
            remote(src, dst, z_send.at[d, k, i], z_recv.at[d, k, i], where)
            for i, (src, dst) in enumerate(zip(source, held))
        ]

    def pair_copies(event, origin, first):
        held, source = block(origin, low, first)
        return [
            remote(src, dst, p_send.at[event, i], p_recv.at[event, i], pair)
            for i, (src, dst) in enumerate(zip(source, held))
        ]

    def mine(origin):
        return lax.rem(origin + group, 2) == 0

    def start_pair(event, origin, first):
        weights, rows = pair_copies(event, origin, first)
        pl.when(mine(origin))(weights.start)
        rows.start()

    def twin_copy(event, origin):
        held = w_out.at[:, 2 * origin + 1 - low]
        return remote(held, held, g_send.at[event], g_recv.at[event], twin)

    def core_copy(event, origin, side, first):
        held, source = block(origin, side, first)
        return remote(source[1], held[1], c_send.at[event], c_recv.at[event], core)

    events = line_events(count)

    def origin_of(event):
        return high if event is None else high - signs[event[0]] * (event[1] + 1)

    def sends_on(d, k):
        return inside(high - signs[d] * k) & inside(high + signs[d])

    def gets(event):
        d, k = event
        return inside(high - signs[d]) & inside(high - signs[d] * (k + 1))

    def start_line(d, k):
        @pl.when(sends_on(d, k))
        def _():
            for copy in line_copies(d, k):
                copy.start()

    for d in (0, 1):
        start_line(d, 0)
    start_pair(0, high, True)
    for copy in across:
        copy.start()
    core_copy(0, high, low, True).start()
    for copy in local:
        copy.start()
    for number, event in enumerate(events[1:], 1):
        d, k = event

        @pl.when(gets(event))
        def _():
            origin = origin_of(event)
            held, _ = block(origin, low, False)
            for i, ref in enumerate(held):
                remote(ref, ref, z_send.at[d, k, i], z_recv.at[d, k, i], pair).wait_recv()
            if k + 1 < count - 1:

                @pl.when(inside(high + signs[d]))
                def _():
                    for copy in line_copies(d, k + 1):
                        copy.start()

            start_pair(number, origin, False)
            core_copy(number, origin, low, False).start()

    def finish(number, event):
        origin = origin_of(event)
        held, _ = block(origin, 1 - low, False)

        def pass_on():
            ref = held[0]
            remote(ref, ref, p_send.at[number, 0], p_recv.at[number, 0], pair).wait_recv()
            twin_copy(number, origin).start()

        pl.when(mine(origin))(pass_on)
        ref = held[1]
        remote(ref, ref, p_send.at[number, 1], p_recv.at[number, 1], pair).wait_recv()
        core_copy(len(events) + number, origin, 1 - low, False).start()

    def drain(number, event):
        origin = origin_of(event)
        weights, rows = pair_copies(number, origin, event is None)
        rows.wait_send()

        def sent():
            weights.wait_send()
            twin_copy(number, origin).wait_send()

        pl.when(mine(origin))(sent)
        pl.when(jnp.logical_not(mine(origin)))(twin_copy(number, origin).wait_recv)
        for place, side in ((number, low), (len(events) + number, 1 - low)):
            copy = core_copy(place, origin, side, event is None and side is low)
            copy.wait_send()
            theirs = s_out.at[:, 2 * origin + side, 1 - seq]
            remote(theirs, theirs, c_send.at[place], c_recv.at[place], core).wait_recv()

    for act in (finish, drain):
        for number, event in enumerate(events):
            if event is None:
                act(number, event)
            else:
                pl.when(gets(event))(functools.partial(act, number, event))
    for d in (0, 1):
        for k in range(count - 1):

            @pl.when(sends_on(d, k))
            def _():
                for copy in line_copies(d, k):
                    copy.wait_send()

    for i, copy in enumerate(across):
        copy.wait_send()
        theirs = x_out.at[1 - seq, pl.ds(0, rows_c) if i == 0 else pl.ds(rows_c, rows_p)]
        remote(theirs, theirs, x_sem.at[0, i], x_sem.at[1, i], core).wait_recv()
    for copy in local:
        copy.wait()


def gather_start(w_own, s_own, cont_rows, prompt_rows):
    chips = lax.axis_size("fsdp")
    count = chips // 2
    events = len(line_events(count))
    rows = cont_rows.shape[0] + prompt_rows.shape[0]
    dma = pltpu.SemaphoreType.DMA
    vmem = pl.BlockSpec(memory_space=pltpu.VMEM)
    kinds, depth, width = w_own.shape
    return pl.pallas_call(
        gather_kernel,
        out_shape=(
            jax.ShapeDtypeStruct((kinds, chips, depth, width), BF),
            jax.ShapeDtypeStruct((2, chips, 2) + s_own.shape[1:], BF),
            jax.ShapeDtypeStruct((2, rows, cont_rows.shape[1]), BF),
        ),
        in_specs=[vmem] * 4,
        out_specs=[vmem] * 3,
        scratch_shapes=[
            dma((4,)),
            dma((2, 2)),
            dma((2, count - 1, 2)),
            dma((2, count - 1, 2)),
            dma((events, 2)),
            dma((events, 2)),
            dma((events,)),
            dma((events,)),
            dma((2 * events,)),
            dma((2 * events,)),
        ],
        compiler_params=pltpu.CompilerParams(collective_id=0, has_side_effects=True),
        name="gather_start",
    )(w_own, s_own, cont_rows, prompt_rows)


def exchange(value):
    return lax.all_to_all(value, "seq", split_axis=0, concat_axis=0, tiled=True)


def on_device(
    prompt_in,
    cont_in,
    enc_in,
    prefix,
    cot_prompt,
    cot_cont,
    w_qkv,
    w_attn_out,
    w_cross_q,
    w_cross_kv,
    w_cross_out,
    w_ffn_in,
    w_ffn_out,
    norm_gain,
    norm_bias,
):
    seq = lax.axis_index("seq")
    width = w_qkv.shape[1] // 3
    hg = width // 2
    shard = w_qkv.shape[0]
    rows_p = prompt_in.shape[1]
    count = cont_in.shape[1]
    half = cont_in.shape[2]
    rows_c = count * half
    reach = prefix[0]

    own = lax.dynamic_index_in_dim(w_qkv.reshape(shard, 3, 2, hg), seq, 2, False).swapaxes(0, 1)
    pair = jnp.stack([prompt_in[0], enc_in[0]], 0)
    wq, shared, x_all = gather_start(own, pair, cont_in[0].reshape(rows_c, width), prompt_in[0])
    wq = wq.reshape(3, -1, hg)
    prompt_all = shared[0].reshape(-1, width)
    enc_all = shared[1].reshape(-1, width)
    norms = jnp.concatenate([norm_gain, norm_bias], 0).T
    norms = jnp.pad(norms, ((0, 0), (0, 128 - norms.shape[1])))
    mixed = jnp.concatenate([w_attn_out, w_cross_q, w_cross_out, w_cross_kv, norms], 1)
    mixed, x_all = lax.optimization_barrier((mixed, x_all))
    mixed = gather_rows(mixed)
    wo = mixed[:, :width]
    wcq = mixed[:, width : 2 * width]
    wco = mixed[:, 2 * width : 3 * width]
    wckv = mixed[:, 3 * width : 5 * width]
    norms = mixed[:, 5 * width :].astype(F32).T
    w_ffn_in, w_ffn_out, x_all = lax.optimization_barrier((w_ffn_in, w_ffn_out, x_all))
    w1 = gather_rows(w_ffn_in)
    w2 = gather_rows(w_ffn_out)

    mine = jnp.concatenate([cont_in[0].reshape(rows_c, width), prompt_in[0]], 0)
    flat = x_all.reshape(-1, width)
    joined = tuple(mm(flat, w).astype(BF).reshape(2, -1, hg) for w in wq)
    prompt_kv = (mm(prompt_all, wq[1]).astype(BF), mm(prompt_all, wq[2]).astype(BF))
    info = jnp.concatenate([reach, lax.axis_index("fsdp")[None] * (2 * rows_p)])
    att, sums = self_forward(joined, prompt_kv, info, half, count, rows_p)
    att_rows = exchange(att)
    proj = mm(att_rows[0], wo[:hg]) + mm(att_rows[1], wo[hg:])
    hat1, scale1 = norm_stats(mine.astype(F32) + proj)
    first = hat1 * norms[0] + norms[3]
    first_low = first.astype(BF)
    cq = mm(first_low, wcq).astype(BF)
    enc_kv = mm(enc_all, wckv).astype(BF)
    cross, cross_sum = cross_forward(cq, enc_kv, rows_c)
    hat2, scale2 = norm_stats(first + mm(cross, wco))
    second = hat2 * norms[1] + norms[4]
    second_low = second.astype(BF)
    pre = mm(second_low, w1)
    gate = 0.5 * (1.0 + lax.erf(pre * 0.7071067811865476))
    act = (pre * gate).astype(BF)
    slope = (gate + pre * jnp.exp(-0.5 * pre * pre) * 0.3989422804014327).astype(BF)
    hat3, scale3 = norm_stats(second + mm(act, w2))
    third = (hat3 * norms[2] + norms[5]).astype(BF)

    cot = jnp.concatenate([cot_cont[0].reshape(rows_c, width), cot_prompt[0]], 0).astype(F32)
    grad3, gain3, bias3 = norm_back(cot, hat3, scale3, norms[2])
    low3 = grad3.astype(BF)
    g_w2 = mm_tn(act, low3).astype(BF)
    grad_pre = (mm_nt(low3, w2) * slope.astype(F32)).astype(BF)
    g_w1 = mm_tn(second_low, grad_pre).astype(BF)
    owners = 2 * lax.axis_size("fsdp")
    columns = [slice(i, i + width) for i in range(0, g_w1.shape[1], width)]
    g_ffn = per_owner([g_w2] + [g_w1[:, cols] for cols in columns])
    grad_pre, g_ffn = lax.optimization_barrier((grad_pre, g_ffn))
    g_ffn = scatter_sum(g_ffn)
    grad_second = grad3 + mm_nt(grad_pre, w1)
    grad2, gain2, bias2 = norm_back(grad_second, hat2, scale2, norms[1])
    low2 = grad2.astype(BF)
    g_wco = mm_tn(cross, low2)
    grad_cross = mm_nt(low2, wco).astype(BF)
    grad_cq, grad_ck, grad_cv = cross_backward(cq, enc_kv, cross, grad_cross, cross_sum, rows_c)
    g_wckv = [mm_tn(enc_all, grad_ck), mm_tn(enc_all, grad_cv)]
    grad_enc = (mm_nt(grad_ck, wckv[:, :width]) + mm_nt(grad_cv, wckv[:, width:])).astype(BF)
    g_wcq = mm_tn(first_low, grad_cq)
    grad_first = grad2 + mm_nt(grad_cq, wcq)
    grad1, gain1, bias1 = norm_back(grad_first, hat1, scale1, norms[0])
    low1 = grad1.astype(BF)
    g_wo = jnp.concatenate([mm_tn(att_rows[0], low1), mm_tn(att_rows[1], low1)], 0)
    g_norms = jnp.stack([gain1, gain2, gain3, bias1, bias2, bias3], 0).astype(BF)
    g_norms = g_norms.reshape(6, owners, shard // 2).swapaxes(0, 1)
    g_norms = jnp.pad(g_norms, ((0, 0), (0, 10), (0, width - shard // 2))).reshape(-1, width)
    g_mixed = [g.astype(BF) for g in (g_wo, g_wcq, g_wco, *g_wckv, grad_enc, g_norms)]
    g_mixed = per_owner(g_mixed)
    grad_att = jnp.stack([mm_nt(low1, wo[:hg]), mm_nt(low1, wo[hg:])], 0).astype(BF)
    grad_att, g_mixed, g_ffn = lax.optimization_barrier((exchange(grad_att), g_mixed, g_ffn))
    g_mixed = scatter_sum(g_mixed)
    grad_joined, grad_pkv = self_backward(
        joined, prompt_kv, info, att, grad_att, sums, half, count, rows_p
    )
    g_q, g_k, g_v = (mm_tn(flat, grad_joined[i].reshape(-1, hg)) for i in range(3))
    g_k = g_k + mm_tn(prompt_all, grad_pkv[0])
    g_v = g_v + mm_tn(prompt_all, grad_pkv[1])
    grad_pr = mm_nt(grad_pkv[0], wq[1]) + mm_nt(grad_pkv[1], wq[2])
    chips = lax.axis_size("fsdp")
    last = [g_q, g_k, g_v, grad_pr[:, :hg], grad_pr[:, hg:]]
    last = jnp.concatenate([v.astype(BF).reshape(chips, -1, hg) for v in last], 1)
    last, g_mixed = lax.optimization_barrier((last.reshape(-1, hg), g_mixed))
    last = lax.psum_scatter(last, "fsdp", scatter_dimension=0, tiled=True)
    q_low, q_high = total_halves(last[: 3 * shard])
    g_qkv = [v.reshape(3, shard, hg) for v in (q_low, q_high)]
    g_qkv = jnp.concatenate([g_qkv[i % 2][i // 2] for i in range(6)], 1).astype(F32)
    grad_x = sum(
        mm_nt(grad_joined[i].reshape(-1, hg), wq[i]) for i in range(3)
    )
    grad_x = grad_x.astype(BF).reshape(x_all.shape)
    cont_x = exchange(grad_x[:, :rows_c])
    grad_in = grad1[:rows_c] + cont_x[0].astype(F32) + cont_x[1].astype(F32)
    grad_pr = last[3 * shard :].reshape(2, 2 * rows_p, hg)
    grad_pr = jnp.concatenate([grad_pr[0], grad_pr[1]], 1).reshape(2, rows_p, width)
    prompt_x = exchange((grad_x[:, rows_c:].astype(F32) + grad_pr.astype(F32)).astype(BF))
    grad_prompt = grad1[rows_c:] + prompt_x[0].astype(F32) + prompt_x[1].astype(F32)

    both = total_halves(g_ffn)
    g_w2 = jnp.concatenate([v[: 2 * shard] for v in both], 0).astype(F32)
    mine = shard // 2
    g_w1 = [
        jnp.concatenate([v[2 * shard + i * mine :][:mine] for i in range(len(columns))], 1)
        for v in both
    ]
    g_w1 = jnp.concatenate(g_w1, 0).astype(F32)
    used = 5 * mine
    grad_enc = g_mixed[used : used + rows_p].astype(F32)
    g_mixed = jnp.concatenate([g_mixed[:used], g_mixed[used + rows_p :]], 0)
    both = total_halves(g_mixed)
    g_wo, g_wcq, g_wco, g_wck, g_wcv = (
        jnp.concatenate([v[i * mine : (i + 1) * mine] for v in both], 0).astype(F32)
        for i in range(5)
    )
    g_norms = jnp.concatenate([v[used : used + 6, :mine] for v in both], 1).astype(F32)
    return (
        third[rows_c:][None],
        third[:rows_c].reshape(cont_in.shape),
        grad_prompt[None],
        grad_in.reshape(cont_in.shape),
        grad_enc[None],
        g_qkv,
        g_wo,
        g_wcq,
        jnp.concatenate([g_wck, g_wcv], 1),
        g_wco,
        g_w1,
        g_w2,
        g_norms[:3],
        g_norms[3:],
    )


def solution(mesh):
    rows = P("grp", ("fsdp", "seq"), None)
    conts = P("grp", "fsdp", "seq", None)
    weight = P("fsdp", None)
    norm = P(None, "fsdp")
    return jax.shard_map(
        on_device,
        mesh=mesh,
        in_specs=(rows, conts, rows, P("grp", "fsdp"), rows, conts) + (weight,) * 7 + (norm,) * 2,
        out_specs=(rows, conts, rows, conts, rows) + (weight,) * 7 + (norm,) * 2,
        check_vma=False,
    )
```

```python
import functools

import jax
import jax.numpy as jnp
from jax import lax
from jax.experimental import pallas as pl
from jax.experimental.pallas import tpu as pltpu
from jax.sharding import PartitionSpec as P

HEAD_DIM = 64
SCALE = 0.125
EPS = 1e-05
MASKED = -1e30
BF = jnp.bfloat16
PAIR = 2 * HEAD_DIM
FLAGS = object()
MESH = pl.DeviceIdType.MESH
F32 = jnp.float32


def mm(a, b):
    return jnp.dot(a, b, preferred_element_type=F32)


def mm_tn(a, b):
    return lax.dot_general(a, b, (((0,), (0,)), ((), ())), preferred_element_type=F32)


def mm_nt(a, b):
    return lax.dot_general(a, b, (((1,), (1,)), ((), ())), preferred_element_type=F32)


def swap(value, axis):
    return lax.ppermute(value, axis, [(0, 1), (1, 0)])


def half_rows(value):
    half = value.shape[0] // 2
    return lax.dynamic_slice_in_dim(value, lax.axis_index("seq") * half, half, 0)


def gather_rows(half):
    return lax.all_gather(half, ("fsdp", "seq"), axis=0, tiled=True)


def scatter_sum(value):
    return lax.psum_scatter(value, ("fsdp", "seq"), scatter_dimension=0, tiled=True)


def per_owner(values):
    owners = 2 * lax.axis_size("fsdp")
    width = values[0].shape[-1]
    pieces = [v.reshape(owners, -1, width) for v in values]
    return jnp.concatenate(pieces, 1).reshape(-1, width)


def total_halves(part):
    across = [(i, 3 - i) for i in range(4)]
    terms = (part, swap(part, "grp")), (swap(part, "seq"), lax.ppermute(part, ("grp", "seq"), across))
    mine, other = ((a.astype(F32) + b.astype(F32)).astype(BF) for a, b in terms)
    first = lax.axis_index("seq") == 0
    return jnp.where(first, mine, other), jnp.where(first, other, mine)


def norm_stats(resid):
    average = jnp.mean(resid, axis=-1, keepdims=True)
    centred = resid - average
    variance = jnp.mean(centred * centred, axis=-1, keepdims=True)
    scale = lax.rsqrt(variance + EPS)
    return centred * scale, scale


def norm_back(grad, hat, scale, gain):
    weighted = grad * gain
    first = jnp.mean(weighted, axis=-1, keepdims=True)
    second = jnp.mean(weighted * hat, axis=-1, keepdims=True)
    back = scale * (weighted - first - hat * second)
    return back, jnp.sum(grad * hat, axis=0), jnp.sum(grad, axis=0)


def dot_nn(a, b):
    return lax.dot_general(a, b, (((1,), (0,)), ((), ())), preferred_element_type=F32)


def dot_nt(a, b):
    return lax.dot_general(a, b, (((1,), (1,)), ((), ())), preferred_element_type=F32)


def lane_masks():
    lane = lax.broadcasted_iota(jnp.int32, (1, 2 * HEAD_DIM), 1)
    low = lane < HEAD_DIM
    return low, jnp.where(low, 1.0, 0.0).astype(BF), jnp.where(low, 0.0, 1.0).astype(BF)


def with_flags(queries):
    lane = lax.broadcasted_iota(jnp.int32, (1, PAIR), 1)
    _, *masks = lane_masks()
    flags = [jnp.where(lane == at, 1.0, 0.0).astype(BF) for at in (HEAD_DIM, 0)]
    return [queries * mask + flag for mask, flag in zip(masks, flags)]


def flag_keys(flagged, keys, limit):
    lane = lax.broadcasted_iota(jnp.int32, keys.shape, 1)
    key = lax.broadcasted_iota(jnp.int32, keys.shape, 0)
    bias = jnp.where(key < limit, 0.0, MASKED)
    for h, at in enumerate((HEAD_DIM, 0)):
        flagged[h] = jnp.where(lane == at, bias, keys.astype(F32)).astype(BF)


def forward_block(queries, segments):
    low, *masks = lane_masks()
    scaled = queries * BF(SCALE)
    outs, sums = [], []
    flagged = with_flags(scaled)
    for h, mask in enumerate(masks):
        own = scaled * mask
        scores = []
        for keys, _, hide in segments:
            part = dot_nt(flagged[h], keys[h]) if hide is FLAGS else dot_nt(own, keys)
            hide = None if hide is FLAGS else hide
            scores.append(part if hide is None else hide(part, 1))
        top = scores[0].max(axis=-1, keepdims=True)
        for part in scores[1:]:
            top = jnp.maximum(top, part.max(axis=-1, keepdims=True))
        total, out = 0.0, 0.0
        for part, (_, values, _) in zip(scores, segments):
            raised = jnp.exp(part - top)
            total = total + raised.sum(axis=-1, keepdims=True)
            out = out + dot_nn(raised.astype(BF), values)
        outs.append(out / total)
        sums.append(top + jnp.log(total))
    out = jnp.where(low, outs[0], outs[1]).astype(BF)
    return out, jnp.where(low, sums[0], sums[1])


def backward_block(queries, grad, out, log_sum, segments):
    _, *masks = lane_masks()
    scaled = queries * BF(SCALE)
    delta = (grad.astype(F32) * out.astype(F32)).T
    owns = [scaled * mask for mask in masks]
    grads = [grad * mask for mask in masks]
    own_pair = jnp.concatenate(owns, 0)
    flagged = with_flags(scaled)
    grad_pair = jnp.concatenate(grads, 0)
    grad_q = [0.0, 0.0]
    grad_kv = []
    for keys, turned, values, hide in segments:
        probs, slopes = [], []
        for h in range(2):
            span = slice(h * HEAD_DIM, (h + 1) * HEAD_DIM)
            scores = dot_nt(keys[h], flagged[h]) if hide is FLAGS else dot_nt(keys, owns[h])
            if hide is not None and hide is not FLAGS:
                scores = hide(scores, 0)
            prob = jnp.exp(scores - log_sum[h : h + 1])
            grad_prob = dot_nt(values, grads[h])
            slope = prob * (grad_prob - delta[span].sum(axis=0, keepdims=True))
            slope = slope.astype(BF)
            grad_q[h] = grad_q[h] + dot_nn(turned[span], slope)
            probs.append(prob.astype(BF))
            slopes.append(slope)
        grad_kv.append(
            (
                dot_nn(jnp.concatenate(slopes, 1), own_pair),
                dot_nn(jnp.concatenate(probs, 1), grad_pair),
            )
        )
    grad_q = jnp.concatenate(grad_q, 0).T * SCALE
    return grad_q.astype(BF), grad_kv


def hide_future(start):
    def hide(scores, axis):
        key = lax.broadcasted_iota(jnp.int32, scores.shape, axis)
        query = lax.broadcasted_iota(jnp.int32, scores.shape, 1 - axis)
        return jnp.where(key <= query + start, scores, MASKED)

    return hide


def store_sums(ref, log_sum):
    turned = log_sum.T
    ref[0, 0, 0:1, : turned.shape[1]] = turned[0:1]
    ref[0, 0, 1:2, : turned.shape[1]] = turned[HEAD_DIM : HEAD_DIM + 1]


def own_spans(pos, block, half):
    spans = []
    for j in range(pos + 1):
        spans.append((j * block // half, j * block % half, block, j == pos))
    merged = []
    for span in spans:
        if merged and not span[3] and merged[-1][0] == span[0]:
            last = merged.pop()
            span = (last[0], last[1], last[2] + span[2], False)
        merged.append(span)
    return merged


def self_forward_kernel(
    info, q_ref, k_ref, v_ref, pk_ref, pv_ref, out_ref, sum_ref, flagged, *, half, count, rows_p, block
):
    step = pl.program_id(1)
    per = 2 * half // block
    for pos in range(per):

        @pl.when((step < count * per) & (lax.rem(step, per) == pos))
        def _():
            c = lax.div(step, per)
            base = pl.multiple_of(c * half, half)
            if pos == 0:
                flag_keys(flagged, pk_ref[...], info[c])
            segments = [((flagged[0], flagged[1]), pv_ref[...], FLAGS)]
            for source, offset, size, last in own_spans(pos, block, half):
                rows = pl.ds(base + offset, size)
                segments.append(
                    (k_ref[source, rows, :], v_ref[source, rows, :], hide_future(0) if last else None)
                )
            rows = pl.ds(base + pos * block % half, block)
            source = pos * block // half
            out, log_sum = forward_block(q_ref[source, rows, :], segments)
            out_ref[source, rows, :] = out
            store_sums(sum_ref, log_sum)

    @pl.when(step == count * per)
    def _():
        rows = slice(count * half, count * half + rows_p)
        queries = jnp.concatenate([q_ref[0, rows, :], q_ref[1, rows, :]], 0)
        out, log_sum = forward_block(queries, [(pk_ref[...], pv_ref[...], hide_future(info[count]))])
        out_ref[0, rows, :] = out[:rows_p]
        out_ref[1, rows, :] = out[rows_p:]
        store_sums(sum_ref, log_sum)


def self_backward_kernel(
    info,
    q_ref,
    k_ref,
    v_ref,
    pk_ref,
    pv_ref,
    out_ref,
    grad_ref,
    sum_ref,
    joined_ref,
    prompt_ref,
    acc_pk,
    acc_pv,
    acc_k,
    acc_v,
    turned_p,
    turned,
    flagged,
    *,
    half,
    count,
    rows_p,
    block,
):
    step = pl.program_id(1)
    per = 2 * half // block

    @pl.when(step == 0)
    def _():
        acc_pk[...] = jnp.zeros_like(acc_pk)
        acc_pv[...] = jnp.zeros_like(acc_pv)
        turned_p[...] = pk_ref[...].T

    for pos in range(per):

        @pl.when((step < count * per) & (lax.rem(step, per) == pos))
        def _():
            c = lax.div(step, per)
            base = pl.multiple_of(c * half, half)
            if pos == 0:
                flag_keys(flagged, pk_ref[...], info[c])
                for source in range(2):
                    turned[:, source * half : (source + 1) * half] = k_ref[
                        source, pl.ds(base, half), :
                    ].T
            spans = own_spans(pos, block, half)
            segments = [((flagged[0], flagged[1]), turned_p[...], pv_ref[...], FLAGS)]
            for source, offset, size, last in spans:
                rows = pl.ds(base + offset, size)
                at = source * half + offset
                segments.append(
                    (
                        k_ref[source, rows, :],
                        turned[:, at : at + size],
                        v_ref[source, rows, :],
                        hide_future(0) if last else None,
                    )
                )
            rows = pl.ds(base + pos * block % half, block)
            source = pos * block // half
            grad_q, grad_kv = backward_block(
                q_ref[source, rows, :],
                grad_ref[source, rows, :],
                out_ref[source, rows, :],
                sum_ref[0, 0],
                segments,
            )
            joined_ref[0, source, rows, :] = grad_q
            acc_pk[...] += grad_kv[0][0]
            acc_pv[...] += grad_kv[0][1]
            for (source, offset, size, last), (grad_k, grad_v) in zip(spans, grad_kv[1:]):
                at = source * half + offset
                if last:
                    acc_k[at : at + size] = grad_k
                    acc_v[at : at + size] = grad_v
                else:
                    acc_k[at : at + size] += grad_k
                    acc_v[at : at + size] += grad_v
            if pos == per - 1:
                for source in range(2):
                    rows = pl.ds(base, half)
                    span = slice(source * half, (source + 1) * half)
                    joined_ref[1, source, rows, :] = acc_k[span].astype(BF)
                    joined_ref[2, source, rows, :] = acc_v[span].astype(BF)

    @pl.when(step == count * per)
    def _():
        rows = slice(count * half, count * half + rows_p)
        both = [jnp.concatenate([r[0, rows, :], r[1, rows, :]], 0) for r in (q_ref, grad_ref, out_ref)]
        grad_q, grad_kv = backward_block(
            *both,
            sum_ref[0, 0][:, : 2 * rows_p],
            [(pk_ref[...], turned_p[...], pv_ref[...], hide_future(info[count]))],
        )
        for source in range(2):
            joined_ref[0, source, rows, :] = grad_q[source * rows_p : (source + 1) * rows_p]
            zero = jnp.zeros((rows_p, grad_q.shape[1]), BF)
            joined_ref[1, source, rows, :] = zero
            joined_ref[2, source, rows, :] = zero
        prompt_ref[0] = (acc_pk[...] + grad_kv[0][0]).astype(BF)
        prompt_ref[1] = (acc_pv[...] + grad_kv[0][1]).astype(BF)


BLOCK = 512


def wide(rows, at, lead=()):
    shape = lead + (rows, PAIR)
    zeros = (0,) * (len(lead) + 1)
    return pl.BlockSpec(shape, lambda pair, step, *_: zeros + (at + pair,))


def sums_spec(block):
    return pl.BlockSpec((1, 1, 8, block), lambda pair, step, *_: (pair, step, 0, 0))


def cost(flops, exps, *arrays):
    return pl.CostEstimate(
        flops=flops,
        transcendentals=exps,
        bytes_accessed=sum(a.size * a.dtype.itemsize for a in arrays),
    )


def self_forward(joined, prompt_kv, info, half, count, rows_p):
    rows, width = joined[0].shape[1:]
    keys = prompt_kv[0].shape[0]
    pairs = width // PAIR
    block = min(BLOCK, half)
    steps = count * 2 * half // block + 1
    scores = 2 * pairs * (count * 2 * half * (keys + half) + 2 * rows_p * keys)
    return pl.pallas_call(
        functools.partial(self_forward_kernel, half=half, count=count, rows_p=rows_p, block=block),
        out_shape=(
            jax.ShapeDtypeStruct((2, rows, width), BF),
            jax.ShapeDtypeStruct((pairs, steps, 8, block), F32),
        ),
        grid_spec=pltpu.PrefetchScalarGridSpec(
            num_scalar_prefetch=1,
            grid=(pairs, steps),
            in_specs=[
                wide(rows, 0, (2,)),
                wide(rows, 0, (2,)),
                wide(rows, 0, (2,)),
                wide(keys, 0),
                wide(keys, 0),
            ],
            out_specs=[wide(rows, 0, (2,)), sums_spec(block)],
            scratch_shapes=[pltpu.VMEM((2, keys, PAIR), BF)],
        ),
        cost_estimate=cost(scores * 512, scores, *joined, *prompt_kv),
        name="self_forward",
    )(info, *joined, *prompt_kv)


def self_backward(joined, prompt_kv, info, out, grad, sums, half, count, rows_p):
    rows, width = joined[0].shape[1:]
    keys = prompt_kv[0].shape[0]
    pairs = width // PAIR
    block = min(BLOCK, half)
    steps = count * 2 * half // block + 1
    scores = 2 * pairs * (count * 2 * half * (keys + half) + 2 * rows_p * keys)
    return pl.pallas_call(
        functools.partial(self_backward_kernel, half=half, count=count, rows_p=rows_p, block=block),
        out_shape=(
            jax.ShapeDtypeStruct((3, 2, rows, width), BF),
            jax.ShapeDtypeStruct((2, keys, width), BF),
        ),
        grid_spec=pltpu.PrefetchScalarGridSpec(
            num_scalar_prefetch=1,
            grid=(pairs, steps),
            in_specs=[
                wide(rows, 0, (2,)),
                wide(rows, 0, (2,)),
                wide(rows, 0, (2,)),
                wide(keys, 0),
                wide(keys, 0),
                wide(rows, 0, (2,)),
                wide(rows, 0, (2,)),
                sums_spec(block),
            ],
            out_specs=[wide(rows, 0, (3, 2)), wide(keys, 0, (2,))],
            scratch_shapes=[pltpu.VMEM((keys, PAIR), F32)] * 2
            + [pltpu.VMEM((2 * half, PAIR), F32)] * 2
            + [pltpu.VMEM((PAIR, keys), BF), pltpu.VMEM((PAIR, 2 * half), BF)]
            + [pltpu.VMEM((2, keys, PAIR), BF)],
        ),
        cost_estimate=cost(scores * 1280, scores, *joined, *prompt_kv, out, grad, *joined),
        name="self_backward",
    )(info, *joined, *prompt_kv, out, grad, sums)


def cross_forward_kernel(q_ref, k_ref, v_ref, out_ref, sum_ref, *, full, rest, block):
    step = pl.program_id(1)

    @pl.when(step < full)
    def _():
        rows = pl.ds(pl.multiple_of(step * block, block), block)
        out, log_sum = forward_block(q_ref[rows, :], [(k_ref[...], v_ref[...], None)])
        out_ref[rows, :] = out
        store_sums(sum_ref, log_sum)

    @pl.when(step == full)
    def _():
        rows = slice(full * block, full * block + rest)
        out, log_sum = forward_block(q_ref[rows, :], [(k_ref[...], v_ref[...], None)])
        out_ref[rows, :] = out
        store_sums(sum_ref, log_sum)


def cross_backward_kernel(
    q_ref, k_ref, v_ref, out_ref, grad_ref, sum_ref, gq_ref, gk_ref, gv_ref, acc_k, acc_v, turned, *, full, rest, block
):
    step = pl.program_id(1)

    @pl.when(step == 0)
    def _():
        acc_k[...] = jnp.zeros_like(acc_k)
        acc_v[...] = jnp.zeros_like(acc_v)
        turned[...] = k_ref[...].T

    def piece(rows, size):
        grad_q, grad_kv = backward_block(
            q_ref[rows, :],
            grad_ref[rows, :],
            out_ref[rows, :],
            sum_ref[0, 0][:, :size],
            [(k_ref[...], turned[...], v_ref[...], None)],
        )
        gq_ref[rows, :] = grad_q
        return grad_kv[0]

    @pl.when(step < full)
    def _():
        grad_k, grad_v = piece(pl.ds(pl.multiple_of(step * block, block), block), block)
        acc_k[...] += grad_k
        acc_v[...] += grad_v

    @pl.when(step == full)
    def _():
        grad_k, grad_v = piece(slice(full * block, full * block + rest), rest)
        gk_ref[...] = (acc_k[...] + grad_k).astype(BF)
        gv_ref[...] = (acc_v[...] + grad_v).astype(BF)


def cross_forward(queries, enc_kv, rows_c):
    rows, width = queries.shape
    keys = enc_kv.shape[0]
    pairs = width // PAIR
    full = rows_c // BLOCK
    scores = 2 * pairs * rows * keys
    return pl.pallas_call(
        functools.partial(cross_forward_kernel, full=full, rest=rows - rows_c, block=BLOCK),
        out_shape=(
            jax.ShapeDtypeStruct((rows, width), BF),
            jax.ShapeDtypeStruct((pairs, full + 1, 8, BLOCK), F32),
        ),
        grid=(pairs, full + 1),
        in_specs=[wide(rows, 0), wide(keys, 0), wide(keys, pairs)],
        out_specs=[wide(rows, 0), sums_spec(BLOCK)],
        cost_estimate=cost(scores * 512, scores, queries, enc_kv),
        name="cross_forward",
    )(queries, enc_kv, enc_kv)


def cross_backward(queries, enc_kv, out, grad, sums, rows_c):
    rows, width = queries.shape
    keys = enc_kv.shape[0]
    pairs = width // PAIR
    full = rows_c // BLOCK
    scores = 2 * pairs * rows * keys
    return pl.pallas_call(
        functools.partial(cross_backward_kernel, full=full, rest=rows - rows_c, block=BLOCK),
        out_shape=(
            jax.ShapeDtypeStruct((rows, width), BF),
            jax.ShapeDtypeStruct((keys, width), BF),
            jax.ShapeDtypeStruct((keys, width), BF),
        ),
        grid=(pairs, full + 1),
        in_specs=[
            wide(rows, 0),
            wide(keys, 0),
            wide(keys, pairs),
            wide(rows, 0),
            wide(rows, 0),
            sums_spec(BLOCK),
        ],
        out_specs=[wide(rows, 0), wide(keys, 0), wide(keys, 0)],
        scratch_shapes=[pltpu.VMEM((keys, PAIR), F32)] * 2 + [pltpu.VMEM((PAIR, keys), BF)],
        cost_estimate=cost(scores * 1280, scores, queries, enc_kv, out, grad),
        name="cross_backward",
    )(queries, enc_kv, enc_kv, out, grad, sums)


def line_events(count):
    return [None] + [(d, k) for k in range(count - 1) for d in (0, 1)]


def gather_kernel(
    w_ref, s_ref, c_ref, p_ref, w_out, s_out, x_out, own, x_sem, z_send, z_recv, p_send, p_recv, g_send, g_recv, c_send, c_recv
):
    f, seq = lax.axis_index("fsdp"), lax.axis_index("seq")
    count = w_out.shape[1] // 2
    high, low = lax.div(f, 2), lax.rem(f, 2)
    pair = {"fsdp": f + 1 - 2 * low}
    core = {"seq": 1 - seq}
    group = lax.axis_index("grp")
    twin = {"grp": 1 - group}
    signs = (1, -1)

    def inside(place):
        return (place >= 0) & (place < count)

    barrier = pltpu.get_barrier_semaphore()
    for where in (pair, core, twin):
        pl.semaphore_signal(barrier, inc=1, device_id=where, device_id_type=MESH)
    for sign in signs:

        @pl.when(inside(high + sign))
        def _():
            pl.semaphore_signal(
                barrier, inc=1, device_id={"fsdp": f + 2 * sign}, device_id_type=MESH
            )

    edges = jnp.where(high > 0, 1, 0) + jnp.where(high < count - 1, 1, 0)
    pl.semaphore_wait(barrier, 3 + edges)

    def remote(src, dst, send, recv, where):
        return pltpu.make_async_remote_copy(
            src_ref=src, dst_ref=dst, send_sem=send, recv_sem=recv, device_id=where, device_id_type=MESH
        )

    rows_c = c_ref.shape[0]
    rows_p = p_ref.shape[0]
    places = [x_out.at[seq, pl.ds(0, rows_c)], x_out.at[seq, pl.ds(rows_c, rows_p)]]
    across = [
        remote(src, dst, x_sem.at[0, i], x_sem.at[1, i], core)
        for i, (src, dst) in enumerate(zip((c_ref, p_ref), places))
    ]
    local = [
        pltpu.make_async_copy(w_ref, w_out.at[:, f], own.at[0]),
        pltpu.make_async_copy(s_ref, s_out.at[:, f, seq], own.at[1]),
        pltpu.make_async_copy(c_ref, places[0], own.at[2]),
        pltpu.make_async_copy(p_ref, places[1], own.at[3]),
    ]

    def block(origin, side, first):
        index = 2 * origin + side
        held = (w_out.at[:, index], s_out.at[:, index, seq])
        return held, ((w_ref, s_ref) if first else held)

    def line_copies(d, k):
        held, source = block(high - signs[d] * k, low, k == 0)
        where = {"fsdp": f + 2 * signs[d]}
        return [
            remote(src, dst, z_send.at[d, k, i], z_recv.at[d, k, i], where)
            for i, (src, dst) in enumerate(zip(source, held))
        ]

    def pair_copies(event, origin, first):
        held, source = block(origin, low, first)
        return [
            remote(src, dst, p_send.at[event, i], p_recv.at[event, i], pair)
            for i, (src, dst) in enumerate(zip(source, held))
        ]

    def mine(origin):
        return lax.rem(origin + group, 2) == 0

    def twin_copy(event, origin):
        held = w_out.at[:, 2 * origin + 1 - low]
        return remote(held, held, g_send.at[event], g_recv.at[event], twin)

    def core_copy(event, origin, side, first):
        held, source = block(origin, side, first)
        return remote(source[1], held[1], c_send.at[event], c_recv.at[event], core)

    events = line_events(count)

    def origin_of(event):
        return high if event is None else high - signs[event[0]] * (event[1] + 1)

    def sends_on(d, k):
        return inside(high - signs[d] * k) & inside(high + signs[d])

    def gets(event):
        d, k = event
        return inside(high - signs[d]) & inside(high - signs[d] * (k + 1))

    def start_line(d, k):
        @pl.when(sends_on(d, k))
        def _():
            for copy in line_copies(d, k):
                copy.start()

    for d in (0, 1):
        start_line(d, 0)
    weights, rows = pair_copies(0, high, True)
    pl.when(mine(high))(weights.start)
    rows.start()
    for copy in across:
        copy.start()
    core_copy(0, high, low, True).start()
    for copy in local:
        copy.start()
    for number, event in enumerate(events[1:], 1):
        d, k = event

        @pl.when(gets(event))
        def _():
            origin = origin_of(event)
            held, _ = block(origin, low, False)
            to_pair = pair_copies(number, origin, False)
            for i, ref in enumerate(held):
                remote(ref, ref, z_send.at[d, k, i], z_recv.at[d, k, i], pair).wait_recv()
                if k + 1 < count - 1:
                    pl.when(inside(high + signs[d]))(line_copies(d, k + 1)[i].start)
                if i == 0:
                    pl.when(mine(origin))(to_pair[0].start)
                else:
                    to_pair[1].start()
            core_copy(number, origin, low, False).start()

    def finish(number, event):
        origin = origin_of(event)
        held, _ = block(origin, 1 - low, False)

        def pass_on():
            ref = held[0]
            remote(ref, ref, p_send.at[number, 0], p_recv.at[number, 0], pair).wait_recv()
            twin_copy(number, origin).start()

        pl.when(mine(origin))(pass_on)
        ref = held[1]
        remote(ref, ref, p_send.at[number, 1], p_recv.at[number, 1], pair).wait_recv()
        core_copy(len(events) + number, origin, 1 - low, False).start()

    def drain(number, event):
        origin = origin_of(event)
        weights, rows = pair_copies(number, origin, event is None)
        rows.wait_send()

        def sent():
            weights.wait_send()
            twin_copy(number, origin).wait_send()

        pl.when(mine(origin))(sent)
        pl.when(jnp.logical_not(mine(origin)))(twin_copy(number, origin).wait_recv)
        for place, side in ((number, low), (len(events) + number, 1 - low)):
            copy = core_copy(place, origin, side, event is None and side is low)
            copy.wait_send()
            theirs = s_out.at[:, 2 * origin + side, 1 - seq]
            remote(theirs, theirs, c_send.at[place], c_recv.at[place], core).wait_recv()

    for act in (finish, drain):
        for number, event in enumerate(events):
            if event is None:
                act(number, event)
            else:
                pl.when(gets(event))(functools.partial(act, number, event))
    for d in (0, 1):
        for k in range(count - 1):

            @pl.when(sends_on(d, k))
            def _():
                for copy in line_copies(d, k):
                    copy.wait_send()

    for i, copy in enumerate(across):
        copy.wait_send()
        theirs = x_out.at[1 - seq, pl.ds(0, rows_c) if i == 0 else pl.ds(rows_c, rows_p)]
        remote(theirs, theirs, x_sem.at[0, i], x_sem.at[1, i], core).wait_recv()
    for copy in local:
        copy.wait()


def gather_start(w_own, s_own, cont_rows, prompt_rows):
    chips = lax.axis_size("fsdp")
    count = chips // 2
    events = len(line_events(count))
    rows = cont_rows.shape[0] + prompt_rows.shape[0]
    dma = pltpu.SemaphoreType.DMA
    vmem = pl.BlockSpec(memory_space=pltpu.VMEM)
    kinds, depth, width = w_own.shape
    return pl.pallas_call(
        gather_kernel,
        out_shape=(
            jax.ShapeDtypeStruct((kinds, chips, depth, width), BF),
            jax.ShapeDtypeStruct((2, chips, 2) + s_own.shape[1:], BF),
            jax.ShapeDtypeStruct((2, rows, cont_rows.shape[1]), BF),
        ),
        in_specs=[vmem] * 4,
        out_specs=[vmem] * 3,
        scratch_shapes=[
            dma((4,)),
            dma((2, 2)),
            dma((2, count - 1, 2)),
            dma((2, count - 1, 2)),
            dma((events, 2)),
            dma((events, 2)),
            dma((events,)),
            dma((events,)),
            dma((2 * events,)),
            dma((2 * events,)),
        ],
        compiler_params=pltpu.CompilerParams(collective_id=0, has_side_effects=True),
        name="gather_start",
    )(w_own, s_own, cont_rows, prompt_rows)


def exchange(value):
    return lax.all_to_all(value, "seq", split_axis=0, concat_axis=0, tiled=True)


def on_device(
    prompt_in,
    cont_in,
    enc_in,
    prefix,
    cot_prompt,
    cot_cont,
    w_qkv,
    w_attn_out,
    w_cross_q,
    w_cross_kv,
    w_cross_out,
    w_ffn_in,
    w_ffn_out,
    norm_gain,
    norm_bias,
):
    seq = lax.axis_index("seq")
    width = w_qkv.shape[1] // 3
    hg = width // 2
    shard = w_qkv.shape[0]
    rows_p = prompt_in.shape[1]
    count = cont_in.shape[1]
    half = cont_in.shape[2]
    rows_c = count * half
    reach = prefix[0]

    norms = jnp.concatenate([norm_gain, norm_bias], 0).T
    norms = jnp.pad(norms, ((0, 0), (0, 128 - norms.shape[1])))
    early = gather_rows(half_rows(jnp.concatenate([w_attn_out, norms], 1)))
    mixed = half_rows(jnp.concatenate([w_cross_q, w_cross_out, w_cross_kv, w_ffn_in], 1))
    w2 = half_rows(w_ffn_out)
    own = lax.dynamic_index_in_dim(w_qkv.reshape(shard, 3, 2, hg), seq, 2, False).swapaxes(0, 1)
    own, mixed, w2 = lax.optimization_barrier((own, mixed, w2))
    pair = jnp.stack([prompt_in[0], enc_in[0]], 0)
    wq, shared, x_all = gather_start(own, pair, cont_in[0].reshape(rows_c, width), prompt_in[0])
    wq = wq.reshape(3, -1, hg)
    prompt_all = shared[0].reshape(-1, width)
    enc_all = shared[1].reshape(-1, width)
    mixed, w2, x_all = lax.optimization_barrier((mixed, w2, x_all))
    mixed, w2 = gather_rows(mixed), gather_rows(w2)
    wo = early[:, :width]
    norms = early[:, width:].astype(F32).T
    wcq = mixed[:, :width]
    wco = mixed[:, width : 2 * width]
    wckv = mixed[:, 2 * width : 4 * width]
    w1 = mixed[:, 4 * width :]

    mine = jnp.concatenate([cont_in[0].reshape(rows_c, width), prompt_in[0]], 0)
    flat = x_all.reshape(-1, width)
    joined = tuple(mm(flat, w).astype(BF).reshape(2, -1, hg) for w in wq)
    prompt_kv = (mm(prompt_all, wq[1]).astype(BF), mm(prompt_all, wq[2]).astype(BF))
    info = jnp.concatenate([reach, lax.axis_index("fsdp")[None] * (2 * rows_p)])
    att, sums = self_forward(joined, prompt_kv, info, half, count, rows_p)
    att_rows = exchange(att)
    proj = mm(att_rows[0], wo[:hg]) + mm(att_rows[1], wo[hg:])
    hat1, scale1 = norm_stats(mine.astype(F32) + proj)
    first = hat1 * norms[0] + norms[3]
    first_low = first.astype(BF)
    cq = mm(first_low, wcq).astype(BF)
    enc_kv = mm(enc_all, wckv).astype(BF)
    cross, cross_sum = cross_forward(cq, enc_kv, rows_c)
    hat2, scale2 = norm_stats(first + mm(cross, wco))
    second = hat2 * norms[1] + norms[4]
    second_low = second.astype(BF)
    pre = mm(second_low, w1)
    gate = 0.5 * (1.0 + lax.erf(pre * 0.7071067811865476))
    act = (pre * gate).astype(BF)
    slope = (gate + pre * jnp.exp(-0.5 * pre * pre) * 0.3989422804014327).astype(BF)
    hat3, scale3 = norm_stats(second + mm(act, w2))
    third = (hat3 * norms[2] + norms[5]).astype(BF)

    cot = jnp.concatenate([cot_cont[0].reshape(rows_c, width), cot_prompt[0]], 0).astype(F32)
    grad3, gain3, bias3 = norm_back(cot, hat3, scale3, norms[2])
    low3 = grad3.astype(BF)
    g_w2 = mm_tn(act, low3).astype(BF)
    grad_pre = (mm_nt(low3, w2) * slope.astype(F32)).astype(BF)
    g_w1 = mm_tn(second_low, grad_pre).astype(BF)
    owners = 2 * lax.axis_size("fsdp")
    columns = [slice(i, i + width) for i in range(0, g_w1.shape[1], width)]
    g_ffn = per_owner([g_w2] + [g_w1[:, cols] for cols in columns])
    grad_pre, g_ffn = lax.optimization_barrier((grad_pre, g_ffn))
    g_ffn = scatter_sum(g_ffn)
    grad_second = grad3 + mm_nt(grad_pre, w1)
    grad2, gain2, bias2 = norm_back(grad_second, hat2, scale2, norms[1])
    low2 = grad2.astype(BF)
    g_wco = mm_tn(cross, low2)
    grad_cross = mm_nt(low2, wco).astype(BF)
    grad_cq, grad_ck, grad_cv = cross_backward(cq, enc_kv, cross, grad_cross, cross_sum, rows_c)
    g_wckv = [mm_tn(enc_all, grad_ck), mm_tn(enc_all, grad_cv)]
    grad_enc = (mm_nt(grad_ck, wckv[:, :width]) + mm_nt(grad_cv, wckv[:, width:])).astype(BF)
    g_wcq = mm_tn(first_low, grad_cq)
    grad_first = grad2 + mm_nt(grad_cq, wcq)
    grad1, gain1, bias1 = norm_back(grad_first, hat1, scale1, norms[0])
    low1 = grad1.astype(BF)
    g_wo = jnp.concatenate([mm_tn(att_rows[0], low1), mm_tn(att_rows[1], low1)], 0)
    g_norms = jnp.stack([gain1, gain2, gain3, bias1, bias2, bias3], 0).astype(BF)
    g_norms = g_norms.reshape(6, owners, shard // 2).swapaxes(0, 1)
    g_norms = jnp.pad(g_norms, ((0, 0), (0, 10), (0, width - shard // 2))).reshape(-1, width)
    g_mixed = [g.astype(BF) for g in (g_wo, g_wcq, g_wco, *g_wckv, grad_enc, g_norms)]
    g_mixed = per_owner(g_mixed)
    grad_att = jnp.stack([mm_nt(low1, wo[:hg]), mm_nt(low1, wo[hg:])], 0).astype(BF)
    grad_att, g_mixed, g_ffn = lax.optimization_barrier((exchange(grad_att), g_mixed, g_ffn))
    g_mixed = scatter_sum(g_mixed)
    grad_joined, grad_pkv = self_backward(
        joined, prompt_kv, info, att, grad_att, sums, half, count, rows_p
    )
    g_q, g_k, g_v = (mm_tn(flat, grad_joined[i].reshape(-1, hg)) for i in range(3))
    g_k = g_k + mm_tn(prompt_all, grad_pkv[0])
    g_v = g_v + mm_tn(prompt_all, grad_pkv[1])
    grad_pr = mm_nt(grad_pkv[0], wq[1]) + mm_nt(grad_pkv[1], wq[2])
    chips = lax.axis_size("fsdp")
    last = [g_q, g_k, g_v, grad_pr[:, :hg], grad_pr[:, hg:]]
    last = jnp.concatenate([v.astype(BF).reshape(chips, -1, hg) for v in last], 1)
    last, g_mixed = lax.optimization_barrier((last.reshape(-1, hg), g_mixed))
    last = lax.psum_scatter(last, "fsdp", scatter_dimension=0, tiled=True)
    q_low, q_high = total_halves(last[: 3 * shard])
    g_qkv = [v.reshape(3, shard, hg) for v in (q_low, q_high)]
    g_qkv = jnp.concatenate([g_qkv[i % 2][i // 2] for i in range(6)], 1).astype(F32)
    grad_x = sum(
        mm_nt(grad_joined[i].reshape(-1, hg), wq[i]) for i in range(3)
    )
    grad_x = grad_x.astype(BF).reshape(x_all.shape)
    cont_x = exchange(grad_x[:, :rows_c])
    grad_in = grad1[:rows_c] + cont_x[0].astype(F32) + cont_x[1].astype(F32)
    grad_pr = last[3 * shard :].reshape(2, 2 * rows_p, hg)
    grad_pr = jnp.concatenate([grad_pr[0], grad_pr[1]], 1).reshape(2, rows_p, width)
    prompt_x = exchange((grad_x[:, rows_c:].astype(F32) + grad_pr.astype(F32)).astype(BF))
    grad_prompt = grad1[rows_c:] + prompt_x[0].astype(F32) + prompt_x[1].astype(F32)

    both = total_halves(g_ffn)
    g_w2 = jnp.concatenate([v[: 2 * shard] for v in both], 0).astype(F32)
    mine = shard // 2
    g_w1 = [
        jnp.concatenate([v[2 * shard + i * mine :][:mine] for i in range(len(columns))], 1)
        for v in both
    ]
    g_w1 = jnp.concatenate(g_w1, 0).astype(F32)
    used = 5 * mine
    grad_enc = g_mixed[used : used + rows_p].astype(F32)
    g_mixed = jnp.concatenate([g_mixed[:used], g_mixed[used + rows_p :]], 0)
    both = total_halves(g_mixed)
    g_wo, g_wcq, g_wco, g_wck, g_wcv = (
        jnp.concatenate([v[i * mine : (i + 1) * mine] for v in both], 0).astype(F32)
        for i in range(5)
    )
    g_norms = jnp.concatenate([v[used : used + 6, :mine] for v in both], 1).astype(F32)
    return (
        third[rows_c:][None],
        third[:rows_c].reshape(cont_in.shape),
        grad_prompt[None],
        grad_in.reshape(cont_in.shape),
        grad_enc[None],
        g_qkv,
        g_wo,
        g_wcq,
        jnp.concatenate([g_wck, g_wcv], 1),
        g_wco,
        g_w1,
        g_w2,
        g_norms[:3],
        g_norms[3:],
    )


def solution(mesh):
    rows = P("grp", ("fsdp", "seq"), None)
    conts = P("grp", "fsdp", "seq", None)
    weight = P("fsdp", None)
    norm = P(None, "fsdp")
    return jax.shard_map(
        on_device,
        mesh=mesh,
        in_specs=(rows, conts, rows, P("grp", "fsdp"), rows, conts) + (weight,) * 7 + (norm,) * 2,
        out_specs=(rows, conts, rows, conts, rows) + (weight,) * 7 + (norm,) * 2,
        check_vma=False,
    )
```
